128 devices in a mesh: row: 8 (over x, core), col: 16 (over y, z).
Axes of the slice: x: 4, y: 4, z: 4, core: 2. Of those that a mesh axis runs over, the one named last changes fastest.
Arguments:
- coarse_in: bfloat16 [256, 256, 512], P('row', 'col'), may hold values from -6 to 6
- coarse_weight: bfloat16 [27, 64, 64], replicated, may hold values from -0.15625 to 0.15625
- coarse_bias: float32 [64], replicated, may hold values from -3 to 3
- fine_in: bfloat16 [1024, 32768], P(('row', 'col')), may hold values from -6 to 6
- weight_first: bfloat16 [27, 64, 64], replicated, may hold values from -0.15625 to 0.15625
- bias_first: float32 [64], replicated, may hold values from -3 to 3
- weight_second: bfloat16 [27, 64, 64], replicated, may hold values from -0.15625 to 0.15625
- bias_second: float32 [64], replicated, may hold values from -3 to 3
- parent_tile: int32 [1024, 1], P(('row', 'col')), may hold values from 0 to 15; in each aligned block of 8 rows (0 to 7, 8 to 15, ...) at most 2 rows name the same one
- parent_cell: int32 [1024], P(('row', 'col')), may hold values from 0 to 63
- neighbours: int32 [1024, 6], P(('row', 'col')), may hold values from -1 to 1023, as said below
Outputs:
- coarse_out: bfloat16 [256, 256, 512], P('row', 'col')
- fine_out: bfloat16 [1024, 32768], P(('row', 'col'))
The draws below stay inside these ranges and needn't reach their ends.
Inputs may be any that keep to these rules, and one draw needn't show every extreme that they name: neighbours[g, f] is the block across face f of block g (f = 0..5: -x, +x, -y, +y, -z, +z), or -1; the relation is symmetric: if h is across face f of g, g is across the opposite face of h. Blocks of device d are rows d * 8 to d * 8 + 7, devices numbered row-major over (row, col). A block across a z face lies on the same device; across an x face on the same device or on the device of the adjacent row on that side, same col; across a y face on the same device or on the device of the adjacent col on that side, same row. Between a device and each such neighbouring device at most 8 block pairs are linked, and in every draw some pair along row and some pair along col link exactly 8. `parent_tile`: among the 8 blocks of one device at most 2 have their parents in one tile; some device has exactly 2 in some tile.
All inputs are finite; a program needn't handle non-finite values.
Results may differ from the reference program's by a relative error of at most 0.0057.
Values may be sent and summed in bfloat16 or wider, within the bound.
A program may use at most 128 MiB of HBM per device.

```python
import math
import jax
import jax.numpy as jnp
import numpy as np
from jax import lax

CH = 64
CXT = 32
CYT = 16
NZC = 8
BLK = 8
CAPP = 2
CAPF = 8
NXC = 256
NYC = 256
NB = 1024
PCELLS = 64
N_ROW = 8
N_COL = 16


def side_links(key, step_dev, upper_ok, lower_ok, forced_row, forced_col, linking):
    device_count = N_ROW * N_COL
    device_ids = jnp.arange(device_count, dtype=jnp.int32)
    keys_plus, keys_minus, keys_count = jax.random.split(key, 3)
    plus_order = jax.vmap(lambda subkey: jax.random.permutation(subkey, BLK))(jax.random.split(keys_plus, device_count)).astype(jnp.int32)
    minus_order = jax.vmap(lambda subkey: jax.random.permutation(subkey, BLK))(jax.random.split(keys_minus, device_count)).astype(jnp.int32)
    positions = jnp.broadcast_to(jnp.arange(BLK, dtype=jnp.int32)[None, :], (device_count, BLK))
    plus_inverse = jnp.zeros((device_count, BLK), jnp.int32).at[device_ids[:, None], plus_order].set(positions)
    minus_inverse = jnp.zeros((device_count, BLK), jnp.int32).at[device_ids[:, None], minus_order].set(positions)
    if linking:
        outward = jax.random.randint(keys_count, (device_count,), 1, CAPF + 1).astype(jnp.int32)
        forced = forced_row * N_COL + forced_col
        outward = jnp.where(device_ids == forced, CAPF, outward)
        outward = jnp.where(upper_ok, outward, 0)
    else:
        outward = jnp.zeros((device_count,), jnp.int32)
    lower_ids = jnp.clip(device_ids - step_dev, 0, device_count - 1)
    upper_ids = jnp.clip(device_ids + step_dev, 0, device_count - 1)
    inward = jnp.where(lower_ok, outward[lower_ids], 0)
    slot_at = plus_inverse
    crossing = slot_at < outward[:, None]
    target_cross = upper_ids[:, None] * BLK + minus_order[upper_ids[:, None], slot_at]
    partner = slot_at - outward[:, None] + inward[:, None]
    target_local = device_ids[:, None] * BLK + minus_order[device_ids[:, None], jnp.clip(partner, 0, BLK - 1)]
    plus_link = jnp.where(crossing, target_cross, jnp.where(partner < BLK, target_local, -1))
    slot_at = minus_inverse
    crossing = slot_at < inward[:, None]
    target_cross = lower_ids[:, None] * BLK + plus_order[lower_ids[:, None], slot_at]
    partner = slot_at - inward[:, None] + outward[:, None]
    target_local = device_ids[:, None] * BLK + plus_order[device_ids[:, None], jnp.clip(partner, 0, BLK - 1)]
    minus_link = jnp.where(crossing, target_cross, jnp.where(partner < BLK, target_local, -1))
    return (minus_link.astype(jnp.int32), plus_link.astype(jnp.int32))


def draw_neighbours(key, part):
    key_x, key_y, key_z, key_pick = jax.random.split(key, 4)
    device_count = N_ROW * N_COL
    device_ids = jnp.arange(device_count, dtype=jnp.int32)
    rows_of = device_ids // N_COL
    cols_of = device_ids % N_COL
    picked = jax.random.randint(key_pick, (4,), 0, 1 << 20).astype(jnp.int32)
    minus_x, plus_x = side_links(key_x, N_COL, rows_of < N_ROW - 1, rows_of > 0, picked[0] % (N_ROW - 1), picked[1] % N_COL, True)
    minus_y, plus_y = side_links(key_y, 1, cols_of < N_COL - 1, cols_of > 0, picked[2] % N_ROW, picked[3] % (N_COL - 1), True)
    never = device_ids < 0
    minus_z, plus_z = side_links(key_z, 0, never, never, 0, 0, False)
    stacked = jnp.stack([minus_x, plus_x, minus_y, plus_y, minus_z, plus_z], axis=-1)
    return stacked.reshape(device_count * BLK, 6)


def with_ends(values, key, smallest, top_value):
    shape = values.shape
    spot = [jax.random.randint(jax.random.fold_in(key, axis), (), 0, shape[axis]) for axis in range(len(shape))]
    values = values.at[tuple(spot)].set(smallest)
    longest = shape.index(max(shape))
    spot[longest] = (spot[longest] + 1) % shape[longest]
    return values.at[tuple(spot)].set(top_value)


def steps_of(stream_key, dims, cuts, low, largest):
    def one(dim, shards_of):
        heights = jax.random.uniform(jax.random.fold_in(jax.random.fold_in(stream_key, 6), dim), (shards_of,), jnp.float32, low / len(cuts), largest / len(cuts))
        return jnp.repeat(jnp.exp(heights), dims[dim] // shards_of).reshape((-1,) + (1,) * (len(dims) - dim - 1))

    factor_of = one(*cuts[0])
    for cut in cuts[1:]:
        factor_of = factor_of * one(*cut)
    return factor_of


def assign_block(key, own, number, rows, number_of, top, most, skew):
    ranking = jax.random.permutation(key, number_of)
    packed, usual = load_shares(number_of, rows * top, most, skew, True), load_shares(number_of, rows * top, most, skew, False)
    places = jnp.arange(number_of)

    def named(tallies, turn):
        used = int((tallies > 0).sum())
        fixed = max(1, used // 4)
        moved = fixed + (places - fixed + turn * (used - fixed)) % max(1, number_of - fixed)
        return jnp.zeros((number_of,), jnp.int32).at[ranking[jnp.where(places < fixed, places, moved)]].set(jnp.asarray(tallies, jnp.int32))

    tallies = jnp.where(number % 4 == 0, named(packed, number // 4), named(usual, number - number // 4 - 1))
    mixed = jax.random.permutation(jax.random.fold_in(own, 3), number_of)
    source_of, receiver = mixed[0:number_of // 2 * 2:2], mixed[1:number_of // 2 * 2:2]
    slack = jnp.minimum(tallies[source_of] - 1, most - tallies[receiver]) // 2
    slack = jnp.where((source_of == ranking[0]) | (receiver == ranking[0]) | (tallies[receiver] == 0), 0, jnp.maximum(slack, 0))
    moved = jax.random.randint(jax.random.fold_in(own, 4), (number_of // 2,), 0, 1 << 20) % (slack + 1)
    tallies = tallies.at[source_of].add(-moved).at[receiver].add(moved)
    items = jnp.searchsorted(jnp.cumsum(tallies), jnp.arange(rows * top), side="right").astype(jnp.int32)
    listing = items.reshape(top, rows).T
    listing = listing[jax.random.permutation(jax.random.fold_in(own, 1), rows)]
    turn = jax.random.randint(jax.random.fold_in(own, 2), (rows, 1), 0, top)
    return jnp.take_along_axis(listing, (jnp.arange(top)[None, :] + turn) % top, axis=1)


def load_shares(amount, total, bound, skew, full):
    portions = [(1 << 20) // math.isqrt(grade ** skew) + 1 for grade in range(1, amount + 1)]
    largest = bound if full else min(bound, max(-(-total // amount), total * portions[0] // sum(portions)))
    least = 1 if total - largest >= amount - 1 else 0
    given, spare = [largest] + [least] * (amount - 1), total - largest - least * (amount - 1)
    while spare > 0:
        free = [i for i in range(1, amount) if given[i] < largest] or [i for i in range(1, amount) if given[i] < bound]
        whole, budget = sum([portions[i] for i in free]), spare
        for i in free:
            extra = min(bound - given[i], max(1, budget * portions[i] // whole), spare)
            given[i] = given[i] + extra
            spare = spare - extra
    return np.array(given)


def gaussian(stream_key, dims, width, bound, pieces=(), held_as=jnp.bfloat16):
    array = jax.random.normal(stream_key, dims, jnp.float32) * width
    if len(pieces) > 0:
        array = steps_of(stream_key, dims, pieces, -0.22, 0.18) * array
    return jnp.clip(array, min=-bound, max=bound).astype(held_as)


def setup_inputs(seed: int = 0) -> dict:
    splits = jax.random.split(jax.random.key(seed), 12)
    coarse_in = gaussian(splits[0], (NXC, NYC, NZC * CH), 1.0, 6.0, ((0, 8), (1, 16)))
    coarse_weight = gaussian(splits[1], (27, CH, CH), (27 * CH) ** -0.5, 0.15625)
    coarse_bias = gaussian(splits[2], (CH,), 0.5, 3.0, (), jnp.float32)
    fine_in = gaussian(splits[3], (NB, 512 * CH), 1.0, 6.0, ((0, 128),))
    weight_first = gaussian(splits[4], (27, CH, CH), (27 * CH) ** -0.5, 0.15625)
    bias_first = gaussian(splits[5], (CH,), 0.5, 3.0, (), jnp.float32)
    weight_second = gaussian(splits[6], (27, CH, CH), (27 * CH) ** -0.5, 0.15625)
    bias_second = gaussian(splits[7], (CH,), 0.5, 3.0, (), jnp.float32)
    parent_tile_keys = jax.random.split(jax.random.fold_in(splits[8], 1), NB // BLK)
    parent_tile_turns = jax.random.permutation(jax.random.fold_in(splits[8], 3), NB // BLK)
    parent_tile = jax.vmap(lambda own, number: assign_block(jax.random.fold_in(splits[8], 2), own, number, BLK, N_COL, 1, CAPP, 2))(parent_tile_keys, parent_tile_turns).reshape((NB, 1))
    parent_cell = with_ends(jax.random.randint(splits[9], (NB,), 0, PCELLS), jax.random.fold_in(splits[9], 1), 0, PCELLS - 1).astype(jnp.int32)
    neighbours = draw_neighbours(jax.random.fold_in(splits[11], 71), 0)
    return dict(coarse_in=coarse_in, coarse_weight=coarse_weight, coarse_bias=coarse_bias, fine_in=fine_in, weight_first=weight_first, bias_first=bias_first, weight_second=weight_second, bias_second=bias_second, parent_tile=parent_tile, parent_cell=parent_cell, neighbours=neighbours)


def pad_block(interior, face_list):
    members = interior.shape[0]
    padded = jnp.zeros((members, 10, 10, 10, CH), interior.dtype)
    padded = padded.at[:, 1:9, 1:9, 1:9].set(interior)
    padded = padded.at[:, 0, 1:9, 1:9].set(face_list[0])
    padded = padded.at[:, 9, 1:9, 1:9].set(face_list[1])
    padded = padded.at[:, 1:9, 0, 1:9].set(face_list[2])
    padded = padded.at[:, 1:9, 9, 1:9].set(face_list[3])
    padded = padded.at[:, 1:9, 1:9, 0].set(face_list[4])
    padded = padded.at[:, 1:9, 1:9, 9].set(face_list[5])
    return padded


def tap_conv(padded, weights, biases):
    members = padded.shape[0]
    summed = jnp.zeros((members * 512, CH), jnp.float32)
    for shift_x in range(3):
        for shift_y in range(3):
            for shift_z in range(3):
                window = padded[:, shift_x:shift_x + 8, shift_y:shift_y + 8, shift_z:shift_z + 8, :]
                summed = summed + jnp.dot(window.reshape(members * 512, CH), weights[9 * shift_x + 3 * shift_y + shift_z], preferred_element_type=jnp.float32)
    return jnp.maximum(summed + biases, 0.0).astype(jnp.bfloat16).reshape(members, 8, 8, 8, CH)


def coarse_row(padded, weights, biases, start_x):
    window = lax.dynamic_slice_in_dim(padded, start_x, 3, 0)
    span_y = padded.shape[1] - 2
    span_z = padded.shape[2] - 2
    summed = jnp.zeros((span_y * span_z, CH), jnp.float32)
    for shift_x in range(3):
        for shift_y in range(3):
            for shift_z in range(3):
                sliced = window[shift_x, shift_y:shift_y + span_y, shift_z:shift_z + span_z, :].reshape(span_y * span_z, CH)
                summed = summed + jnp.dot(sliced, weights[9 * shift_x + 3 * shift_y + shift_z], preferred_element_type=jnp.float32)
    return jnp.maximum(summed + biases, 0.0).astype(jnp.bfloat16).reshape(span_y, span_z * CH)


def layer_of(volume, direction, layer_index):
    if direction == 0:
        return volume[:, layer_index]
    if direction == 1:
        return volume[:, :, layer_index]
    return volume[:, :, :, layer_index]


def neighbour_faces(volume, neighbours):
    face_list = []
    for facing in range(6):
        layer_index = 7 if facing % 2 == 0 else 0
        source = layer_of(volume, facing // 2, layer_index)
        linked = neighbours[:, facing]
        taken = source[jnp.clip(linked, 0, source.shape[0] - 1)]
        face_list.append(jnp.where((linked >= 0)[:, None, None, None], taken, jnp.zeros_like(taken)))
    return face_list


def fine_conv(volume, neighbours, weights, biases):
    face_list = neighbour_faces(volume, neighbours)
    total_blocks = volume.shape[0]
    width_group = math.gcd(total_blocks, 256)
    groups = total_blocks // width_group
    shaped = (volume.reshape(groups, width_group, 8, 8, 8, CH),) + tuple(face_item.reshape(groups, width_group, 8, 8, CH) for face_item in face_list)

    def one_group(members):
        return tap_conv(pad_block(members[0], members[1:]), weights, biases)

    return lax.map(one_group, shaped).reshape(total_blocks, 8, 8, 8, CH)


def upsample(regions):
    cubes = regions.reshape(regions.shape[0], 4, 4, 4, CH)
    return jnp.repeat(jnp.repeat(jnp.repeat(cubes, 2, axis=1), 2, axis=2), 2, axis=3)


def reference(coarse_in, coarse_weight, coarse_bias, fine_in, weight_first, bias_first, weight_second, bias_second, parent_tile, parent_cell, neighbours):
    coarse_grid = coarse_in.reshape(NXC, NYC, NZC, CH)
    padded = jnp.pad(coarse_grid, ((1, 1), (1, 1), (1, 1), (0, 0)))
    coarse_out = lax.map(lambda start_x: coarse_row(padded, coarse_weight, coarse_bias, start_x), jnp.arange(NXC, dtype=jnp.int32))
    block_ids = jnp.arange(NB, dtype=jnp.int32)
    row_of = (block_ids // BLK) // N_COL
    quarter_y = CYT // 4
    quarter_z = NZC // 4
    corner_x = row_of * CXT + 4 * (parent_cell // (quarter_y * quarter_z))
    corner_y = parent_tile[:, 0] * CYT + 4 * ((parent_cell // quarter_z) % quarter_y)
    corner_z = 4 * CH * (parent_cell % quarter_z)
    regions = jax.vmap(lambda at_x, at_y, at_z: lax.dynamic_slice(coarse_out, (at_x, at_y, at_z), (4, 4, 4 * CH)))(corner_x, corner_y, corner_z)
    upsampled = upsample(regions)
    start_volume = (fine_in.reshape(NB, 8, 8, 8, CH).astype(jnp.float32) + upsampled.astype(jnp.float32)).astype(jnp.bfloat16)
    first_layer = fine_conv(start_volume, neighbours, weight_first, bias_first)
    second_layer = fine_conv(first_layer, neighbours, weight_second, bias_second)
    return coarse_out, second_layer.reshape(NB, 512 * CH)
```

```python
import functools
import jax
import jax.numpy as jnp
from jax import lax
from jax.experimental import pallas as pl
from jax.experimental.pallas import tpu as pltpu
from jax.sharding import PartitionSpec as P

CH = 64
X = 32
Y = 16
NB = 8
F32 = jnp.float32
BF = jnp.bfloat16
MESH = pl.DeviceIdType.MESH


def lanes(shape):
    return lax.broadcasted_iota(jnp.int32, shape, len(shape) - 1)


def sublanes(shape):
    return lax.broadcasted_iota(jnp.int32, shape, len(shape) - 2)


def build_weights(w, bw):
    zero = jnp.zeros((64, 64), BF)
    wide = jnp.zeros((64, 128), BF)

    def one(k, carry):
        wm, w0, wp = w[3 * k], w[3 * k + 1], w[3 * k + 2]
        a = jnp.concatenate([w0, wm], axis=1)
        b = jnp.concatenate([wp, w0], axis=1)
        c = jnp.concatenate([zero, wp], axis=1)
        d = jnp.concatenate([wm, zero], axis=1)
        for r, (left, right) in enumerate(
            ((a, wide), (b, d), (c, a), (wide, b), (wide, c), (d, wide))
        ):
            bw[k, r * 64 : (r + 1) * 64, 0:128] = left
            bw[k, r * 64 : (r + 1) * 64, 128:256] = right
        return carry

    lax.fori_loop(0, 9, one, 0)


def tile_bias(b, bt):
    for i in range(4):
        bt[:, i * 64 : (i + 1) * 64] = b[...]


def take(v, idx):
    return jnp.concatenate(
        [
            jnp.take_along_axis(v[:, k : k + 128], idx, axis=0, mode="promise_in_bounds")
            for k in range(0, v.shape[1], 128)
        ],
        axis=1,
    )


def pack6(v, zm, zp, low):
    first = jnp.concatenate([v[:, 0:256], jnp.where(low, v[:, 256:384], zm)], axis=1)
    second = jnp.concatenate([v[:, 256:512], jnp.where(low, zp, v[:, 128:256])], axis=1)
    return jnp.concatenate([first, second], axis=0).astype(BF)


def load_cell(s, *at):
    v = s[at].astype(F32)
    return jnp.concatenate([v[0:8], v[8:16]], axis=1)


def body(
    nr,
    nc,
    cin,
    cw,
    cb,
    fin,
    w1,
    b1,
    w2,
    b2,
    ptile,
    pcell,
    nb,
    cout_hbm,
    fout_hbm,
    vin,
    vf,
    vw,
    bw,
    bt,
    edge,
    hx,
    hy,
    hc,
    hf,
    cp,
    cs,
    cout,
    req,
    reqr,
    sel,
    psend,
    precv,
    s1,
    s2,
    fr,
    pad,
    fout,
    lsem,
    hsend,
    hrecv,
    qsend,
    qrecv,
    asend,
    arecv,
    fsend,
    frecv,
):
    r = lax.axis_index("row")
    c = lax.axis_index("col")
    rp, rm = lax.rem(r + 1, nr), lax.rem(r + nr - 1, nr)
    cpl, cmi = lax.rem(c + 1, nc), lax.rem(c + nc - 1, nc)
    me = r * nc + c

    barrier = pltpu.get_barrier_semaphore()
    greet = [(r, lax.rem(c + k, nc)) for k in range(1, nc)]
    greet += [(rp, c), (rm, c), (rp, cpl), (rp, cmi), (rm, cpl), (rm, cmi)]
    for peer in greet:
        pl.semaphore_signal(barrier, inc=1, device_id=peer, device_id_type=MESH)

    loads = [
        pltpu.make_async_copy(cin, vin, lsem.at[0]),
        pltpu.make_async_copy(cw, vw.at[0], lsem.at[1]),
        pltpu.make_async_copy(fin, vf, lsem.at[2]),
        pltpu.make_async_copy(w1, vw.at[1], lsem.at[3]),
        pltpu.make_async_copy(w2, vw.at[2], lsem.at[4]),
    ]
    for copy in loads:
        copy.start()

    tiles = [ptile[b] for b in range(NB)]
    cells = [pcell[b] for b in range(NB)]
    slots = []
    for b in range(NB):
        n = jnp.int32(0)
        for e in range(b):
            n = n + jnp.where(tiles[e] == tiles[b], 1, 0)
        slots.append(n)
    row_id = sublanes((nc * 8, 128))
    wanted = jnp.full((nc * 8, 128), -1, jnp.int32)
    for b in range(NB):
        wanted = jnp.where(row_id == tiles[b] * 8 + slots[b], cells[b], wanted)
    req[...] = wanted.reshape(nc, 8, 128)

    loads[0].wait()
    ei = sublanes((64, 512))
    ej = lanes((64, 512))
    pick = jnp.where(ej == jnp.where(ei < 32, ei * 16 + 15, (ei - 32) * 16), 1.0, 0.0).astype(BF)
    edge[...] = jnp.dot(pick, vin[...].reshape(512, 512), preferred_element_type=F32).astype(BF)

    pl.semaphore_wait(barrier, len(greet))

    halos = []
    for i, (src, dst, peer) in enumerate(
        (
            (edge.at[0:32], hy.at[0], (r, cpl)),
            (edge.at[32:64], hy.at[1], (r, cmi)),
            (vin.at[31], hx.at[0], (rp, c)),
            (vin.at[0], hx.at[1], (rm, c)),
            (edge.at[16:32], hc.at[0], (rp, cpl)),
            (edge.at[48:64], hc.at[1], (rp, cmi)),
            (edge.at[0:16], hc.at[2], (rm, cpl)),
            (edge.at[32:48], hc.at[3], (rm, cmi)),
        )
    ):
        copy = pltpu.make_async_remote_copy(
            src_ref=src,
            dst_ref=dst,
            send_sem=hsend.at[i],
            recv_sem=hrecv.at[i],
            device_id=peer,
            device_id_type=MESH,
        )
        copy.start()
        halos.append(copy)
    asks = []
    for k in range(1, nc):
        d = lax.rem(c + k, nc)
        copy = pltpu.make_async_remote_copy(
            src_ref=req.at[d],
            dst_ref=reqr.at[c],
            send_sem=qsend.at[k],
            recv_sem=qrecv.at[k],
            device_id=(r, d),
            device_id_type=MESH,
        )
        copy.start()
        asks.append(copy)
    reqr[c] = req[c]

    loads[1].wait()
    build_weights(vw.at[0], bw.at[0])
    tile_bias(cb, bt.at[0])
    tile_bias(b1, bt.at[1])
    tile_bias(b2, bt.at[2])

    for copy in halos:
        copy.wait()

    low16 = lanes((16, 128)) < 64
    zero16 = jnp.zeros((16, 128), F32)
    y16 = sublanes((16, 512))
    hf[...] = hy[...].astype(F32)

    def place(at, a, left, right):
        for dy, v in enumerate(
            (
                jnp.where(y16 == 0, left, pltpu.roll(a, 1, 0)),
                a,
                jnp.where(y16 == 15, right, pltpu.roll(a, 15, 0)),
            )
        ):
            o = dy * 384
            cp[at, 0, :, o : o + 256] = v[:, 0:256].astype(BF)
            cp[at, 0, :, o + 256 : o + 384] = jnp.where(low16, v[:, 256:384], zero16).astype(BF)
            cp[at, 1, :, o : o + 256] = v[:, 256:512].astype(BF)
            cp[at, 1, :, o + 256 : o + 384] = jnp.where(low16, zero16, v[:, 128:256]).astype(BF)

    def coarse_one(x, carry):
        left = jnp.where(c > 0, hf[0, pl.ds(x, 1), :], 0.0)
        right = jnp.where(c < nc - 1, hf[1, pl.ds(x, 1), :], 0.0)
        place(x + 1, vin[x].astype(F32), left, right)
        return carry

    lax.fori_loop(0, X, coarse_one, 0)
    for at, ok, i, row, j in ((0, r > 0, 0, 15, 0), (33, r < nr - 1, 1, 0, 2)):
        corner_l = hc[j].astype(F32)[row : row + 1]
        corner_r = hc[j + 1].astype(F32)[row : row + 1]
        place(
            at,
            jnp.where(ok, hx[i].astype(F32), 0.0),
            jnp.where(ok & (c > 0), corner_l, 0.0),
            jnp.where(ok & (c < nc - 1), corner_r, 0.0),
        )

    cbias = bt[0]

    def coarse_conv(i, carry):
        x0 = i * 8
        left = jnp.concatenate(
            [cp[pl.ds(x0 + dx, 8)].reshape(256, 1152) for dx in range(3)], axis=1
        )
        out = jnp.dot(left, bw[0].reshape(3456, 256), preferred_element_type=F32)
        out = jnp.maximum(out + cbias, 0.0).astype(BF).reshape(8, 2, 16, 256)
        cs[pl.ds(x0, 8)] = out
        cout[pl.ds(x0, 8), :, 0:256] = out[:, 0]
        cout[pl.ds(x0, 8), :, 256:512] = out[:, 1]
        return carry

    lax.fori_loop(0, 4, coarse_conv, 0)
    cstore = pltpu.make_async_copy(cout, cout_hbm, lsem.at[5])
    cstore.start()

    for copy in asks:
        copy.wait()
    i16 = sublanes((16, 128))
    l16 = lanes((16, 128))

    def choose(d, carry):
        for s in range(2):
            cell = jnp.broadcast_to(reqr[d, s : s + 1, :], (16, 128))
            px = (cell >> 3) * 4 + (i16 >> 2)
            py = ((cell >> 1) & 3) * 4 + (i16 & 3)
            target = jnp.where(cell >= 0, (px * 2 + (cell & 1)) * 16 + py, -1)
            for k in range(8):
                sel[d, s * 16 : (s + 1) * 16, k * 128 : (k + 1) * 128] = jnp.where(
                    target == l16 + k * 128, 1.0, 0.0
                ).astype(BF)
        return carry

    lax.fori_loop(0, nc, choose, 0)
    psend[...] = (
        jnp.dot(
            sel[...].reshape(nc * 32, 1024),
            cs[...].reshape(1024, 256),
            preferred_element_type=F32,
        )
        .astype(BF)
        .reshape(nc, 32, 256)
    )
    gives = []
    for k in range(1, nc):
        d = lax.rem(c + k, nc)
        copy = pltpu.make_async_remote_copy(
            src_ref=psend.at[d],
            dst_ref=precv.at[c],
            send_sem=asend.at[k],
            recv_sem=arecv.at[k],
            device_id=(r, d),
            device_id_type=MESH,
        )
        copy.start()
        gives.append(copy)
    precv[c] = psend[c]

    loads[3].wait()
    build_weights(vw.at[1], bw.at[1])
    loads[4].wait()
    build_weights(vw.at[2], bw.at[2])
    loads[2].wait()

    b8 = sublanes((8, 128))
    low = lanes((8, 128)) < 64
    index, local, cross = [], [], []
    for f in range(6):
        linked = jnp.full((8, 128), -1, jnp.int32)
        for b in range(NB):
            linked = jnp.where(b8 == b, nb[b, f], linked)
        owner = linked >> 3
        index.append(linked & 7)
        local.append(owner == me)
        other = me + (-nc, nc, -1, 1, -1, 1)[f]
        cross.append((linked >= 0) & (owner == other))

    base = jnp.zeros((8, 128), jnp.int32)
    for b in range(NB):
        base = jnp.where(b8 == b, tiles[b] * 32 + slots[b] * 16, base)
    l8 = lanes((8, 128))
    rows = []
    for q in range(16):
        rows.append(
            jnp.concatenate(
                [
                    jnp.where(base + q == l8 + k * 128, 1.0, 0.0)
                    for k in range(nc * 32 // 128)
                ],
                axis=1,
            )
        )
    sel2 = jnp.concatenate(rows, axis=0).astype(BF)

    for copy in gives:
        copy.wait()
    up = jnp.dot(sel2, precv[...].reshape(nc * 32, 256), preferred_element_type=F32)

    for q in range(16):
        u = up[q * 8 : (q + 1) * 8]
        parts = []
        for k in (0, 128):
            v = u[:, k : k + 128]
            w = pltpu.roll(v, 64, 1)
            parts += [jnp.where(low, v, w), jnp.where(low, w, v)]
        u = jnp.concatenate(parts, axis=1)
        for i in range(2):
            for j in range(2):
                x, y = (q // 4) * 2 + i, (q % 4) * 2 + j
                o = (x * 8 + y) * 512
                v = vf[:, o : o + 512].astype(F32) + u
                s1[x, y] = jnp.concatenate([v[:, 0:256], v[:, 256:512]], axis=0).astype(BF)

    zero8 = jnp.zeros((8, 128), F32)
    corner = jnp.zeros((16, 384), BF)
    for i in (0, 9):
        for j in (0, 9):
            pad[i, j] = corner

    def fine(s, turn, store):
        moves = []
        for i, (src, peer) in enumerate(
            ((s.at[7], (rp, c)), (s.at[0], (rm, c)), (s.at[:, 7], (r, cpl)), (s.at[:, 0], (r, cmi)))
        ):
            copy = pltpu.make_async_remote_copy(
                src_ref=src,
                dst_ref=fr.at[turn, i],
                send_sem=fsend.at[turn, i],
                recv_sem=frecv.at[turn, i],
                device_id=peer,
                device_id_type=MESH,
            )
            copy.start()
            moves.append(copy)

        def inner(x, carry):
            for y in range(8):
                v = load_cell(s, x, y)
                zm = jnp.where(local[4], take(v[:, 384:512], index[4]), 0.0)
                zp = jnp.where(local[5], take(v[:, 0:128], index[5]), 0.0)
                pad[x + 1, y + 1] = pack6(v, zm, zp, low)
            return carry

        lax.fori_loop(0, 8, inner, 0)
        for copy in moves:
            copy.wait()

        def outer(k, carry):
            for f in range(4):
                layer = 7 if f % 2 == 0 else 0
                near = load_cell(s, layer, k) if f < 2 else load_cell(s, k, layer)
                far = load_cell(fr, turn, f, k)
                in_l = jnp.concatenate([local[f]] * 4, axis=1)
                in_c = jnp.concatenate([cross[f]] * 4, axis=1)
                v = jnp.where(
                    in_l, take(near, index[f]), jnp.where(in_c, take(far, index[f]), 0.0)
                )
                edge_at = 0 if f % 2 == 0 else 9
                v = pack6(v, zero8, zero8, low)
                if f < 2:
                    pad[edge_at, k + 1] = v
                else:
                    pad[k + 1, edge_at] = v
            return carry

        lax.fori_loop(0, 8, outer, 0)
        bias = bt[turn + 1]

        def conv(i, carry):
            x0 = i * 2
            left = jnp.concatenate(
                [
                    pad[pl.ds(x0 + dx, 2), dy : dy + 8].reshape(256, 384)
                    for dx in range(3)
                    for dy in range(3)
                ],
                axis=1,
            )
            out = jnp.dot(left, bw[turn + 1].reshape(3456, 256), preferred_element_type=F32)
            store(x0, jnp.maximum(out + bias, 0.0).astype(BF))
            return carry

        lax.fori_loop(0, 4, conv, 0)

    def keep(x0, out):
        s2[pl.ds(x0, 2)] = out.reshape(2, 8, 16, 256)

    def final(x0, out):
        wide = out.astype(F32)
        for i in range(32):
            at = pl.multiple_of(x0 * 4096 + i * 256, 256)
            fout[:, pl.ds(at, 256)] = wide[i * 8 : (i + 1) * 8].astype(BF)

    fine(s1, 0, keep)
    fine(s2, 1, final)
    fstore = pltpu.make_async_copy(fout, fout_hbm, lsem.at[6])
    fstore.start()
    cstore.wait()
    fstore.wait()


def shards(
    coarse_in,
    coarse_weight,
    coarse_bias,
    fine_in,
    weight_first,
    bias_first,
    weight_second,
    bias_second,
    parent_tile,
    parent_cell,
    neighbours,
):
    nr = lax.axis_size("row")
    nc = lax.axis_size("col")
    anywhere = pl.BlockSpec(memory_space=pl.ANY)
    vector = pl.BlockSpec(memory_space=pltpu.VMEM)
    scalar = pl.BlockSpec(memory_space=pltpu.SMEM)
    dma = pltpu.SemaphoreType.DMA
    return pl.pallas_call(
        functools.partial(body, nr, nc),
        out_shape=(
            jax.ShapeDtypeStruct(coarse_in.shape, BF),
            jax.ShapeDtypeStruct(fine_in.shape, BF),
        ),
        in_specs=[
            anywhere,
            anywhere,
            vector,
            anywhere,
            anywhere,
            vector,
            anywhere,
            vector,
            scalar,
            scalar,
            scalar,
        ],
        out_specs=(anywhere, anywhere),
        scratch_shapes=[
            pltpu.VMEM((X, Y, 512), BF),
            pltpu.VMEM((NB, 32768), BF),
            pltpu.VMEM((3, 27, CH, CH), BF),
            pltpu.VMEM((3, 9, 384, 256), BF),
            pltpu.VMEM((3, 1, 256), F32),
            pltpu.VMEM((64, 512), BF),
            pltpu.VMEM((2, 16, 512), BF),
            pltpu.VMEM((2, 32, 512), BF),
            pltpu.VMEM((4, 16, 512), BF),
            pltpu.VMEM((2, 32, 512), F32),
            pltpu.VMEM((34, 2, 16, 1152), BF),
            pltpu.VMEM((X, 2, 16, 256), BF),
            pltpu.VMEM((X, Y, 512), BF),
            pltpu.VMEM((nc, 8, 128), jnp.int32),
            pltpu.VMEM((nc, 8, 128), jnp.int32),
            pltpu.VMEM((nc, 32, 1024), BF),
            pltpu.VMEM((nc, 32, 256), BF),
            pltpu.VMEM((nc, 32, 256), BF),
            pltpu.VMEM((8, 8, 16, 256), BF),
            pltpu.VMEM((8, 8, 16, 256), BF),
            pltpu.VMEM((2, 4, 8, 16, 256), BF),
            pltpu.VMEM((10, 10, 16, 384), BF),
            pltpu.VMEM((NB, 32768), BF),
            dma((7,)),
            dma((8,)),
            dma((8,)),
            dma((nc,)),
            dma((nc,)),
            dma((nc,)),
            dma((nc,)),
            dma((2, 4)),
            dma((2, 4)),
        ],
        compiler_params=pltpu.CompilerParams(collective_id=0, has_side_effects=True),
    )(
        coarse_in,
        coarse_weight,
        coarse_bias.reshape(1, CH),
        fine_in,
        weight_first,
        bias_first.reshape(1, CH),
        weight_second,
        bias_second.reshape(1, CH),
        parent_tile.reshape(NB),
        parent_cell,
        neighbours,
    )


def solution(mesh):
    placed = (
        P("row", "col", None),
        P(),
        P(),
        P(("row", "col"), None),
        P(),
        P(),
        P(),
        P(),
        P(("row", "col"), None),
        P(("row", "col")),
        P(("row", "col"), None),
    )
    return jax.shard_map(
        shards,
        mesh=mesh,
        in_specs=placed,
        out_specs=(P("row", "col", None), P(("row", "col"), None)),
        check_vma=False,
    )
```

```python
import functools
import jax
import jax.numpy as jnp
from jax import lax
from jax.experimental import pallas as pl
from jax.experimental.pallas import tpu as pltpu
from jax.sharding import PartitionSpec as P

CH = 64
X = 32
Y = 16
NB = 8
F32 = jnp.float32
BF = jnp.bfloat16
MESH = pl.DeviceIdType.MESH


def lanes(shape):
    return lax.broadcasted_iota(jnp.int32, shape, len(shape) - 1)


def sublanes(shape):
    return lax.broadcasted_iota(jnp.int32, shape, len(shape) - 2)


def build_weights(w, bw):
    zero = jnp.zeros((64, 64), BF)
    wide = jnp.zeros((64, 128), BF)

    def one(k, carry):
        wm, w0, wp = w[3 * k], w[3 * k + 1], w[3 * k + 2]
        a = jnp.concatenate([w0, wm], axis=1)
        b = jnp.concatenate([wp, w0], axis=1)
        c = jnp.concatenate([zero, wp], axis=1)
        d = jnp.concatenate([wm, zero], axis=1)
        for r, (left, right) in enumerate(
            ((a, wide), (b, d), (c, a), (wide, b), (wide, c), (d, wide))
        ):
            bw[k, r * 64 : (r + 1) * 64, 0:128] = left
            bw[k, r * 64 : (r + 1) * 64, 128:256] = right
        return carry

    lax.fori_loop(0, 9, one, 0)


def tile_bias(b, bt):
    for i in range(4):
        bt[:, i * 64 : (i + 1) * 64] = b[...]


def take(v, idx):
    return jnp.concatenate(
        [
            jnp.take_along_axis(v[:, k : k + 128], idx, axis=0, mode="promise_in_bounds")
            for k in range(0, v.shape[1], 128)
        ],
        axis=1,
    )


def pack6(v, zm, zp, low):
    first = jnp.concatenate([v[:, 0:256], jnp.where(low, v[:, 256:384], zm)], axis=1)
    second = jnp.concatenate([v[:, 256:512], jnp.where(low, zp, v[:, 128:256])], axis=1)
    return jnp.concatenate([first, second], axis=0).astype(BF)


def load_cell(s, *at):
    v = s[at].astype(F32)
    return jnp.concatenate([v[0:8], v[8:16]], axis=1)


def order(nc):
    side = {16: 4, 4: 2}[nc]
    dist = lambda v: min(v, side - v)
    pairs = [(a, b) for a in range(side) for b in range(side)]
    return side, sorted(pairs, key=lambda p: -dist(p[0]) - dist(p[1]))


def body(
    nr,
    nc,
    cin,
    cw,
    cb,
    fin,
    w1,
    b1,
    w2,
    b2,
    ptile,
    pcell,
    nb,
    cout,
    fout,
    vin,
    vf,
    vw,
    bw,
    bt,
    edge,
    hx,
    hy,
    hc,
    yl,
    cp,
    cacc,
    cs,
    req,
    reqr,
    sel,
    psend,
    precv,
    s1,
    s2,
    fr,
    pad,
    facc,
    lsem,
    hsend,
    hrecv,
    qsend,
    qrecv,
    asend,
    arecv,
    fsend,
    frecv,
):
    r = lax.axis_index("row")
    c = lax.axis_index("col")
    rp, rm = lax.rem(r + 1, nr), lax.rem(r + nr - 1, nr)
    cpl, cmi = lax.rem(c + 1, nc), lax.rem(c + nc - 1, nc)
    me = r * nc + c
    side, offsets = order(nc)
    cy, cz = lax.div(c, side), lax.rem(c, side)
    peers = [lax.rem(cy + a, side) * side + lax.rem(cz + b, side) for a, b in offsets]
    barrier = pltpu.get_barrier_semaphore()
    greet = [(r, d) for d in peers[:-1]]
    greet += [(rp, c), (rm, c), (rp, cpl), (rp, cmi), (rm, cpl), (rm, cmi)]
    for peer in greet:
        pl.semaphore_signal(barrier, inc=1, device_id=peer, device_id_type=MESH)

    loads = [
        pltpu.make_async_copy(cin, vin, lsem.at[0]),
        pltpu.make_async_copy(cw, vw.at[0], lsem.at[1]),
        pltpu.make_async_copy(fin, vf, lsem.at[2]),
        pltpu.make_async_copy(w1, vw.at[1], lsem.at[3]),
        pltpu.make_async_copy(w2, vw.at[2], lsem.at[4]),
    ]
    for copy in loads:
        copy.start()
    sends = []

    def send(src, dst, ssem, rsem, peer):
        copy = pltpu.make_async_remote_copy(
            src_ref=src,
            dst_ref=dst,
            send_sem=ssem,
            recv_sem=rsem,
            device_id=peer,
            device_id_type=MESH,
        )
        copy.start()
        sends.append(copy)
        return copy

    tiles = [ptile[b] for b in range(NB)]
    cells = [pcell[b] for b in range(NB)]
    slots = []
    for b in range(NB):
        n = jnp.int32(0)
        for e in range(b):
            n = n + jnp.where(tiles[e] == tiles[b], 1, 0)
        slots.append(n)
    row_id = sublanes((nc * 8, 128))
    wanted = jnp.full((nc * 8, 128), -1, jnp.int32)
    for b in range(NB):
        wanted = jnp.where(row_id == tiles[b] * 8 + slots[b], cells[b], wanted)
    req[...] = wanted.reshape(nc, 8, 128)

    loads[0].wait()
    ei = sublanes((64, 512))
    ej = lanes((64, 512))
    pick = jnp.where(ej == jnp.where(ei < 32, ei * 16 + 15, (ei - 32) * 16), 1.0, 0.0).astype(BF)
    edge[...] = jnp.dot(pick, vin[...].reshape(512, 512), preferred_element_type=F32).astype(BF)
    loads[1].wait()
    build_weights(vw.at[0], bw.at[0])
    tile_bias(cb, bt.at[0])
    tile_bias(b1, bt.at[1])
    tile_bias(b2, bt.at[2])
    pl.semaphore_wait(barrier, len(greet))
    halos = [
        send(src, dst, hsend.at[i], hrecv.at[i], peer)
        for i, (src, dst, peer) in enumerate(
            (
                (edge.at[16:32], hc.at[0], (rp, cpl)),
                (edge.at[48:64], hc.at[1], (rp, cmi)),
                (edge.at[0:16], hc.at[2], (rm, cpl)),
                (edge.at[32:48], hc.at[3], (rm, cmi)),
                (edge.at[0:32], hy.at[0], (r, cpl)),
                (edge.at[32:64], hy.at[1], (r, cmi)),
                (vin.at[31], hx.at[0], (rp, c)),
                (vin.at[0], hx.at[1], (rm, c)),
            )
        )
    ]
    asks = [
        send(req.at[d], reqr.at[c], qsend.at[k], qrecv.at[k], (r, d))
        for k, d in enumerate(peers[:-1])
    ]
    reqr[c] = req[c]

    low16 = lanes((16, 128)) < 64
    zero16 = jnp.zeros((16, 128), F32)
    y16 = sublanes((16, 512))

    def place(at, a, left, right):
        for dy, v in enumerate(
            (
                jnp.where(y16 == 0, left, pltpu.roll(a, 1, 0)),
                a,
                jnp.where(y16 == 15, right, pltpu.roll(a, 15, 0)),
            )
        ):
            o = dy * 384
            cp[at, 0, :, o : o + 256] = v[:, 0:256].astype(BF)
            cp[at, 0, :, o + 256 : o + 384] = jnp.where(low16, v[:, 256:384], zero16).astype(BF)
            cp[at, 1, :, o : o + 256] = v[:, 256:512].astype(BF)
            cp[at, 1, :, o + 256 : o + 384] = jnp.where(low16, zero16, v[:, 128:256]).astype(BF)

    def coarse_one(x, carry):
        place(x + 1, vin[x].astype(F32), 0.0, 0.0)
        return carry

    lax.fori_loop(0, X, coarse_one, 0)
    blank = jnp.zeros((2, 16, 1152), BF)
    cp[0] = blank
    cp[33] = blank
    cbias = bt[0]

    def coarse_conv(i, carry):
        x0 = i * 16
        left = jnp.concatenate(
            [cp[pl.ds(x0 + dx, 16)].reshape(512, 1152) for dx in range(3)], axis=1
        )
        out = jnp.dot(left, bw[0].reshape(3456, 256), preferred_element_type=F32)
        cacc[pl.ds(x0, 16)] = (out + cbias).reshape(16, 2, 16, 256)
        return carry

    lax.fori_loop(0, 2, coarse_conv, 0)

    for copy in asks:
        copy.wait_recv()
    i16 = sublanes((16, 128))
    l16 = lanes((16, 128))
    for k, d in enumerate(peers):
        for s in range(2):
            cell = jnp.broadcast_to(reqr[d, s : s + 1, :], (16, 128))
            px = (cell >> 3) * 4 + (i16 >> 2)
            py = ((cell >> 1) & 3) * 4 + (i16 & 3)
            target = jnp.where(cell >= 0, (px * 2 + (cell & 1)) * 16 + py, -1)
            for j in range(8):
                sel[k, s * 16 : (s + 1) * 16, j * 128 : (j + 1) * 128] = jnp.where(
                    target == l16 + j * 128, 1.0, 0.0
                ).astype(BF)
    for copy in halos:
        copy.wait_recv()

    for at, ok, i, row, j in ((0, r > 0, 0, 15, 0), (33, r < nr - 1, 1, 0, 2)):
        corner_l = hc[j].astype(F32)[row : row + 1]
        corner_r = hc[j + 1].astype(F32)[row : row + 1]
        place(
            at,
            jnp.where(ok, hx[i].astype(F32), 0.0),
            jnp.where(ok & (c > 0), corner_l, 0.0),
            jnp.where(ok & (c < nc - 1), corner_r, 0.0),
        )
    low32 = lanes((32, 128)) < 64
    x32 = sublanes((32, 256))
    for i, ok in enumerate((c > 0, c < nc - 1)):
        v = jnp.where(ok, hy[i].astype(F32), 0.0)
        left = jnp.concatenate(
            [
                jnp.concatenate([v[:, 0:256], jnp.where(low32, v[:, 256:384], 0.0)], axis=1),
                jnp.concatenate([v[:, 256:512], jnp.where(low32, 0.0, v[:, 128:256])], axis=1),
            ],
            axis=0,
        ).astype(BF)
        part = [
            jnp.dot(left, bw[0, 3 * dx + 2 * i], preferred_element_type=F32) for dx in range(3)
        ]
        for g in range(2):
            before, here, after = [p[g * 32 : (g + 1) * 32] for p in part]
            yl[i, g] = (
                here
                + jnp.where(x32 == 0, 0.0, pltpu.roll(before, 1, 0))
                + jnp.where(x32 == 31, 0.0, pltpu.roll(after, 31, 0))
            )
    for at, x, k in ((0, 0, 0), (33, 31, 6)):
        cacc[x] = cacc[x] + jnp.dot(
            cp[at].reshape(32, 1152),
            bw[0, k : k + 3].reshape(1152, 256),
            preferred_element_type=F32,
        ).reshape(2, 16, 256)
    y256 = sublanes((16, 256))

    def coarse_out(x, carry):
        for g in range(2):
            v = cacc[x, g]
            v = v + jnp.where(y256 == 0, yl[0, g, pl.ds(x, 1), :], 0.0)
            v = v + jnp.where(y256 == 15, yl[1, g, pl.ds(x, 1), :], 0.0)
            v = jnp.maximum(v, 0.0).astype(BF)
            cs[x, g] = v
            cout[x, :, g * 256 : (g + 1) * 256] = v
        return carry

    lax.fori_loop(0, X, coarse_out, 0, unroll=2)
    gives = []
    for m in range(0, nc, 4):
        psend[m : m + 4] = (
            jnp.dot(
                sel[m : m + 4].reshape(128, 1024),
                cs[...].reshape(1024, 256),
                preferred_element_type=F32,
            )
            .astype(BF)
            .reshape(4, 32, 256)
        )
        for k in range(m, m + 4):
            if k < nc - 1:
                gives.append(
                    send(psend.at[k], precv.at[c], asend.at[k], arecv.at[k], (r, peers[k]))
                )
    precv[c] = psend[nc - 1]
    loads[3].wait()
    build_weights(vw.at[1], bw.at[1])
    loads[4].wait()
    build_weights(vw.at[2], bw.at[2])
    loads[2].wait()
    b8 = sublanes((8, 128))
    low = lanes((8, 128)) < 64
    index, local, cross = [], [], []
    for f in range(6):
        linked = jnp.full((8, 128), -1, jnp.int32)
        for b in range(NB):
            linked = jnp.where(b8 == b, nb[b, f], linked)
        owner = linked >> 3
        index.append(linked & 7)
        local.append(owner == me)
        other = me + (-nc, nc, -1, 1, -1, 1)[f]
        cross.append((linked >= 0) & (owner == other))

    base = jnp.zeros((8, 128), jnp.int32)
    for b in range(NB):
        base = jnp.where(b8 == b, tiles[b] * 32 + slots[b] * 16, base)
    l8 = lanes((8, 128))
    rows = []
    for q in range(16):
        rows.append(
            jnp.concatenate(
                [
                    jnp.where(base + q == l8 + k * 128, 1.0, 0.0)
                    for k in range(nc * 32 // 128)
                ],
                axis=1,
            )
        )
    sel2 = jnp.concatenate(rows, axis=0).astype(BF)

    zero8 = jnp.zeros((8, 128), F32)
    blank = jnp.zeros((16, 384), BF)
    for turn in range(2):
        for i in range(10):
            for j in range(10):
                if i in (0, 9) or j in (0, 9):
                    pad[turn, i, j] = blank
    for copy in gives:
        copy.wait_recv()
    up = jnp.dot(sel2, precv[...].reshape(nc * 32, 256), preferred_element_type=F32)
    grown = []
    for q in range(16):
        u = up[q * 8 : (q + 1) * 8]
        parts = []
        for k in (0, 128):
            v = u[:, k : k + 128]
            w = pltpu.roll(v, 64, 1)
            parts += [jnp.where(low, v, w), jnp.where(low, w, v)]
        grown.append(jnp.concatenate(parts, axis=1))

    def begin(x, y):
        o = (x * 8 + y) * 512
        v = vf[:, o : o + 512].astype(F32) + grown[(x // 2) * 4 + y // 2]
        s1[x, y] = jnp.concatenate([v[:, 0:256], v[:, 256:512]], axis=0).astype(BF)

    def send_y(s, turn):
        return [
            send(s.at[:, 7], fr.at[turn, 2], fsend.at[turn, 2], frecv.at[turn, 2], (r, cpl)),
            send(s.at[:, 0], fr.at[turn, 3], fsend.at[turn, 3], frecv.at[turn, 3], (r, cmi)),
        ]

    def send_x(s, turn):
        return [
            send(s.at[7], fr.at[turn, 0], fsend.at[turn, 0], frecv.at[turn, 0], (rp, c)),
            send(s.at[0], fr.at[turn, 1], fsend.at[turn, 1], frecv.at[turn, 1], (rm, c)),
        ]

    inside = range(1, 7)
    for x in range(8):
        begin(x, 0)
        begin(x, 7)
    ymoves = send_y(s1, 0)
    for y in inside:
        begin(0, y)
        begin(7, y)
    moves = send_x(s1, 0) + ymoves
    for x in inside:
        for y in inside:
            begin(x, y)

    def fine_main(s, turn):
        def inner(x, carry):
            for y in range(8):
                v = load_cell(s, x, y)
                zm = jnp.where(local[4], take(v[:, 384:512], index[4]), 0.0)
                zp = jnp.where(local[5], take(v[:, 0:128], index[5]), 0.0)
                pad[turn, x + 1, y + 1] = pack6(v, zm, zp, low)
            return carry

        lax.fori_loop(0, 8, inner, 0)
        bias = bt[turn + 1]

        def conv(i, carry):
            x0 = i * 4
            left = jnp.concatenate(
                [
                    pad[turn, pl.ds(x0 + dx, 4), dy : dy + 8].reshape(512, 384)
                    for dx in range(3)
                    for dy in range(3)
                ],
                axis=1,
            )
            out = jnp.dot(left, bw[turn + 1].reshape(3456, 256), preferred_element_type=F32)
            facc[pl.ds(x0, 4)] = (out + bias).reshape(4, 8, 16, 256)
            return carry

        lax.fori_loop(0, 2, conv, 0)

    def fine_fix(s, turn, moves):
        for f in range(4):
            moves[f].wait_recv()
            layer, at, tap = (7, 0, 0) if f % 2 == 0 else (0, 9, 2)
            in_l = jnp.concatenate([local[f]] * 4, axis=1)
            in_c = jnp.concatenate([cross[f]] * 4, axis=1)
            for k in range(8):
                near = load_cell(s, layer, k) if f < 2 else load_cell(s, k, layer)
                far = load_cell(fr, turn, f, k)
                v = jnp.where(
                    in_l, take(near, index[f]), jnp.where(in_c, take(far, index[f]), 0.0)
                )
                v = pack6(v, zero8, zero8, low)
                if f < 2:
                    pad[turn, at, k + 1] = v
                else:
                    pad[turn, k + 1, at] = v
            if f < 2:
                left = [pad[turn, at, d : d + 8].reshape(128, 384) for d in range(3)]
                right = bw[turn + 1, 3 * tap : 3 * tap + 3].reshape(1152, 256)
            else:
                left = [pad[turn, d : d + 8, at].reshape(128, 384) for d in range(3)]
                right = jnp.concatenate([bw[turn + 1, 3 * d + tap] for d in range(3)], axis=0)
            add = jnp.dot(
                jnp.concatenate(left, axis=1), right, preferred_element_type=F32
            ).reshape(8, 16, 256)
            if f < 2:
                facc[7 - layer] = facc[7 - layer] + add
            else:
                facc[:, 7 - layer] = facc[:, 7 - layer] + add

    def keep(x, y):
        s2[x, y] = jnp.maximum(facc[x, y], 0.0).astype(BF)

    def final(x, y):
        v = jnp.maximum(facc[x, y], 0.0)
        at = pl.multiple_of((x * 8 + y) * 512, 512)
        fout[:, pl.ds(at, 512)] = jnp.concatenate([v[0:8], v[8:16]], axis=1).astype(BF)

    def each_inside(put):
        def one(x, carry):
            for y in inside:
                put(x, y)
            return carry

        lax.fori_loop(1, 7, one, 0)

    fine_main(s1, 0)
    each_inside(keep)
    fine_fix(s1, 0, moves)
    for x in range(8):
        keep(x, 0)
        keep(x, 7)
    ymoves = send_y(s2, 1)
    for y in inside:
        keep(0, y)
        keep(7, y)
    moves = send_x(s2, 1) + ymoves
    fine_main(s2, 1)
    each_inside(final)
    fine_fix(s2, 1, moves)
    for x in range(8):
        final(x, 0)
        final(x, 7)
    for y in inside:
        final(0, y)
        final(7, y)
    for copy in sends:
        copy.wait_send()


def put_out(coarse, fine, coarse_hbm, fine_hbm, sem):
    copies = [
        pltpu.make_async_copy(coarse, coarse_hbm, sem.at[0]),
        pltpu.make_async_copy(fine, fine_hbm, sem.at[1]),
    ]
    for copy in copies:
        copy.start()
    for copy in copies:
        copy.wait()


def shards(
    coarse_in,
    coarse_weight,
    coarse_bias,
    fine_in,
    weight_first,
    bias_first,
    weight_second,
    bias_second,
    parent_tile,
    parent_cell,
    neighbours,
):
    nr = lax.axis_size("row")
    nc = lax.axis_size("col")
    anywhere = pl.BlockSpec(memory_space=pl.ANY)
    vector = pl.BlockSpec(memory_space=pltpu.VMEM)
    scalar = pl.BlockSpec(memory_space=pltpu.SMEM)
    dma = pltpu.SemaphoreType.DMA
    coarse, fine = pl.pallas_call(
        functools.partial(body, nr, nc),
        out_shape=(pltpu.VMEM(coarse_in.shape, BF), pltpu.VMEM(fine_in.shape, BF)),
        in_specs=[anywhere, anywhere, vector, anywhere, anywhere, vector, anywhere, vector]
        + [scalar] * 3,
        out_specs=(vector, vector),
        scratch_shapes=[
            pltpu.VMEM((X, Y, 512), BF),
            pltpu.VMEM((NB, 32768), BF),
            pltpu.VMEM((3, 27, CH, CH), BF),
            pltpu.VMEM((3, 9, 384, 256), BF),
            pltpu.VMEM((3, 1, 256), F32),
            pltpu.VMEM((64, 512), BF),
            pltpu.VMEM((2, 16, 512), BF),
            pltpu.VMEM((2, 32, 512), BF),
            pltpu.VMEM((4, 16, 512), BF),
            pltpu.VMEM((2, 2, 32, 256), F32),
            pltpu.VMEM((34, 2, 16, 1152), BF),
            pltpu.VMEM((X, 2, 16, 256), F32),
            pltpu.VMEM((X, 2, 16, 256), BF),
            pltpu.VMEM((nc, 8, 128), jnp.int32),
            pltpu.VMEM((nc, 8, 128), jnp.int32),
            pltpu.VMEM((nc, 32, 1024), BF),
            pltpu.VMEM((nc, 32, 256), BF),
            pltpu.VMEM((nc, 32, 256), BF),
            pltpu.VMEM((8, 8, 16, 256), BF),
            pltpu.VMEM((8, 8, 16, 256), BF),
            pltpu.VMEM((2, 4, 8, 16, 256), BF),
            pltpu.VMEM((2, 10, 10, 16, 384), BF),
            pltpu.VMEM((8, 8, 16, 256), F32),
            dma((5,)),
            dma((8,)),
            dma((8,)),
            dma((nc,)),
            dma((nc,)),
            dma((nc,)),
            dma((nc,)),
            dma((2, 4)),
            dma((2, 4)),
        ],
        compiler_params=pltpu.CompilerParams(collective_id=0, has_side_effects=True),
    )(
        coarse_in,
        coarse_weight,
        coarse_bias.reshape(1, CH),
        fine_in,
        weight_first,
        bias_first.reshape(1, CH),
        weight_second,
        bias_second.reshape(1, CH),
        parent_tile.reshape(NB),
        parent_cell,
        neighbours,
    )
    return pl.pallas_call(
        put_out,
        out_shape=(
            jax.ShapeDtypeStruct(coarse_in.shape, BF),
            jax.ShapeDtypeStruct(fine_in.shape, BF),
        ),
        in_specs=[anywhere, anywhere],
        out_specs=(anywhere, anywhere),
        scratch_shapes=[dma((2,))],
        compiler_params=pltpu.CompilerParams(vmem_limit_bytes=1 << 20),
    )(coarse, fine)


def solution(mesh):
    placed = (
        P("row", "col", None),
        P(),
        P(),
        P(("row", "col"), None),
        P(),
        P(),
        P(),
        P(),
        P(("row", "col"), None),
        P(("row", "col")),
        P(("row", "col"), None),
    )
    return jax.shard_map(
        shards,
        mesh=mesh,
        in_specs=placed,
        out_specs=(P("row", "col", None), P(("row", "col"), None)),
        check_vma=False,
    )
```

```python
import functools
import jax
import jax.numpy as jnp
from jax import lax
from jax.experimental import pallas as pl
from jax.experimental.pallas import tpu as pltpu
from jax.sharding import PartitionSpec as P

CH = 64
X = 32
Y = 16
NB = 8
PARTS = 2
F32 = jnp.float32
BF = jnp.bfloat16
MESH = pl.DeviceIdType.MESH


def lanes(shape):
    return lax.broadcasted_iota(jnp.int32, shape, len(shape) - 1)


def sublanes(shape):
    return lax.broadcasted_iota(jnp.int32, shape, len(shape) - 2)


def build_weights(w, bw):
    zero = jnp.zeros((64, 64), BF)
    wide = jnp.zeros((64, 128), BF)

    def one(k, carry):
        wm, w0, wp = w[3 * k], w[3 * k + 1], w[3 * k + 2]
        a = jnp.concatenate([w0, wm], axis=1)
        b = jnp.concatenate([wp, w0], axis=1)
        c = jnp.concatenate([zero, wp], axis=1)
        d = jnp.concatenate([wm, zero], axis=1)
        for r, (left, right) in enumerate(
            ((a, wide), (b, d), (c, a), (wide, b), (wide, c), (d, wide))
        ):
            bw[k, r * 64 : (r + 1) * 64, 0:128] = left
            bw[k, r * 64 : (r + 1) * 64, 128:256] = right
        return carry

    lax.fori_loop(0, 9, one, 0)


def tile_bias(b, bt):
    for i in range(4):
        bt[:, i * 64 : (i + 1) * 64] = b[...]


def take(v, idx):
    return jnp.concatenate(
        [
            jnp.take_along_axis(v[:, k : k + 128], idx, axis=0, mode="promise_in_bounds")
            for k in range(0, v.shape[1], 128)
        ],
        axis=1,
    )


def pack6(v, zm, zp, low):
    first = jnp.concatenate([v[:, 0:256], jnp.where(low, v[:, 256:384], zm)], axis=1)
    second = jnp.concatenate([v[:, 256:512], jnp.where(low, zp, v[:, 128:256])], axis=1)
    return jnp.concatenate([first, second], axis=0).astype(BF)


def load_cell(s, *at):
    v = s[at].astype(F32)
    return jnp.concatenate([v[0:8], v[8:16]], axis=1)


def order(nc):
    side = {16: 4, 4: 2}[nc]
    dist = lambda v: min(v, side - v)
    pairs = [(a, b) for a in range(side) for b in range(side)]
    return side, sorted(pairs, key=lambda p: -dist(p[0]) - dist(p[1]))


def body(
    nr,
    nc,
    cin,
    cw,
    cb,
    fin,
    w1,
    b1,
    w2,
    b2,
    ptile_in,
    pcell_in,
    nb_in,
    cout,
    fout,
    ptile,
    pcell,
    nb,
    braw,
    vin,
    vf,
    vw,
    bw,
    bt,
    edge,
    crn,
    hx,
    hy,
    hc,
    yl,
    cp,
    cacc,
    cs,
    req,
    reqr,
    sel,
    psend,
    precv,
    s1,
    s2,
    fr,
    pad,
    facc,
    lsem,
    hsend,
    hrecv,
    asem,
    gsem,
    frecv,
):
    r = lax.axis_index("row")
    c = lax.axis_index("col")
    me = r * nc + c
    side, offsets = order(nc)
    cy, cz = lax.div(c, side), lax.rem(c, side)
    peers = [lax.rem(cy + a, side) * side + lax.rem(cz + b, side) for a, b in offsets]
    up, down, right, left = r < nr - 1, r > 0, c < nc - 1, c > 0
    barrier = pltpu.get_barrier_semaphore()
    near = [
        ((r, c + 1), right),
        ((r, c - 1), left),
        ((r + 1, c), up),
        ((r - 1, c), down),
        ((r + 1, c + 1), up & right),
        ((r + 1, c - 1), up & left),
        ((r - 1, c + 1), down & right),
        ((r - 1, c - 1), down & left),
    ]
    heard = jnp.int32(nc - 1)
    for d in peers[:-1]:
        pl.semaphore_signal(barrier, inc=1, device_id=(r, d), device_id_type=MESH)
    for peer, there in near[2:]:
        heard = heard + jnp.where(there, 1, 0)

        @pl.when(there)
        def _(peer=peer):
            pl.semaphore_signal(barrier, inc=1, device_id=peer, device_id_type=MESH)

    loads = [
        pltpu.make_async_copy(cin, vin, lsem.at[0]),
        pltpu.make_async_copy(ptile_in, ptile, lsem.at[5]),
        pltpu.make_async_copy(pcell_in, pcell, lsem.at[6]),
        pltpu.make_async_copy(cw, vw.at[0], lsem.at[1]),
        pltpu.make_async_copy(nb_in, nb, lsem.at[7]),
        pltpu.make_async_copy(cb, braw.at[0], lsem.at[8]),
        pltpu.make_async_copy(b1, braw.at[1], lsem.at[9]),
        pltpu.make_async_copy(b2, braw.at[2], lsem.at[10]),
        pltpu.make_async_copy(fin, vf, lsem.at[2]),
        pltpu.make_async_copy(w1, vw.at[1], lsem.at[3]),
        pltpu.make_async_copy(w2, vw.at[2], lsem.at[4]),
    ]
    lin, ltile, lcell, lcw, lnb, lb0, lb1, lb2, lfin, lw1, lw2 = loads
    for copy in loads:
        copy.start()

    def remote(src, dst, ssem, rsem, peer):
        return pltpu.make_async_remote_copy(
            src_ref=src,
            dst_ref=dst,
            send_sem=ssem,
            recv_sem=rsem,
            device_id=peer,
            device_id_type=MESH,
        )

    def start(copy, there):
        @pl.when(there)
        def _():
            copy.start()

    def sent(copy, there):
        @pl.when(there)
        def _():
            copy.wait_send()

    def came(copy, there):
        @pl.when(there)
        def _():
            copy.wait_recv()
    ltile.wait()
    lcell.wait()
    tiles = [ptile[b] for b in range(NB)]
    cells = [pcell[b] for b in range(NB)]
    slots = []
    for b in range(NB):
        n = jnp.int32(0)
        for e in range(b):
            n = n + jnp.where(tiles[e] == tiles[b], 1, 0)
        slots.append(n)
    row_id = sublanes((nc, 128))
    wanted = jnp.zeros((nc, 128), jnp.int32)
    for b in range(NB):
        ask = (cells[b] + 1) * jnp.where(slots[b] == 0, 1, 128)
        wanted = wanted + jnp.where(row_id == tiles[b], ask, 0)
    for t in range(nc):
        req[t] = wanted[t : t + 1]

    lin.wait()
    ei = sublanes((64, 512))
    ej = lanes((64, 512))
    pick = jnp.where(ej == jnp.where(ei < 32, ei * 16 + 15, (ei - 32) * 16), 1.0, 0.0).astype(BF)
    found = jnp.dot(pick, vin[...].reshape(512, 512), preferred_element_type=F32)
    edge[...] = found.astype(BF)
    for i, row in enumerate((31, 63, 0, 32)):
        crn[i] = found[row : row + 1]
    lcw.wait()
    build_weights(vw.at[0], bw.at[0])
    lb0.wait()
    lb1.wait()
    lb2.wait()
    for i in range(3):
        tile_bias(braw.at[i], bt.at[i])
    pl.semaphore_wait(barrier, heard)
    for d in peers[:-1]:
        remote(req.at[d], reqr.at[c], asem.at[0], asem.at[1], (r, d)).start()
    asks = remote(
        req.at[pl.ds(0, nc - 1)],
        reqr.at[pl.ds(0, nc - 1)],
        asem.at[0],
        asem.at[1],
        (r, peers[0]),
    )
    halos = []
    for i, (src, dst, to, frm) in enumerate(
        (
            (crn.at[0], hc.at[0], 4, 7),
            (crn.at[1], hc.at[1], 5, 6),
            (crn.at[2], hc.at[2], 6, 5),
            (crn.at[3], hc.at[3], 7, 4),
            (edge.at[0:32], hy.at[0], 0, 1),
            (edge.at[32:64], hy.at[1], 1, 0),
            (vin.at[31], hx.at[0], 2, 3),
            (vin.at[0], hx.at[1], 3, 2),
        )
    ):
        copy = remote(src, dst, hsend.at[i], hrecv.at[i], near[to][0])
        start(copy, near[to][1])
        halos.append((copy, near[to][1], near[frm][1]))
    reqr[c] = req[c]

    low16 = lanes((16, 128)) < 64
    zero16 = jnp.zeros((16, 128), F32)
    y16 = sublanes((16, 512))

    def place(at, a, left, right):
        for dy, v in enumerate(
            (
                jnp.where(y16 == 0, left, pltpu.roll(a, 1, 0)),
                a,
                jnp.where(y16 == 15, right, pltpu.roll(a, 15, 0)),
            )
        ):
            o = dy * 384
            cp[at, 0, :, o : o + 256] = v[:, 0:256].astype(BF)
            cp[at, 0, :, o + 256 : o + 384] = jnp.where(low16, v[:, 256:384], zero16).astype(BF)
            cp[at, 1, :, o : o + 256] = v[:, 256:512].astype(BF)
            cp[at, 1, :, o + 256 : o + 384] = jnp.where(low16, zero16, v[:, 128:256]).astype(BF)

    def coarse_one(x, carry):
        place(x + 1, vin[x].astype(F32), 0.0, 0.0)
        return carry

    lax.fori_loop(0, X, coarse_one, 0)
    blank = jnp.zeros((2, 16, 1152), BF)
    cp[0] = blank
    cp[33] = blank
    cbias = bt[0]

    def coarse_conv(i, carry):
        x0 = i * 16
        left = jnp.concatenate(
            [cp[pl.ds(x0 + dx, 16)].reshape(512, 1152) for dx in range(3)], axis=1
        )
        out = jnp.dot(left, bw[0].reshape(3456, 256), preferred_element_type=F32)
        cacc[pl.ds(x0, 16)] = (out + cbias).reshape(16, 2, 16, 256)
        return carry

    lax.fori_loop(0, 2, coarse_conv, 0)

    asks.wait_recv()
    i16 = sublanes((16, 128))
    l16 = lanes((16, 128))
    for k, d in enumerate(peers):
        both = jnp.broadcast_to(reqr[d], (16, 128))
        for s in range(2):
            cell = ((both >> (7 * s)) & 127) - 1
            px = (cell >> 3) * 4 + (i16 >> 2)
            py = ((cell >> 1) & 3) * 4 + (i16 & 3)
            target = jnp.where(cell >= 0, (px * 2 + (cell & 1)) * 16 + py, -1)
            for j in range(8):
                sel[k, s * 16 : (s + 1) * 16, j * 128 : (j + 1) * 128] = jnp.where(
                    target == l16 + j * 128, 1.0, 0.0
                ).astype(BF)
    for copy, _, there in halos:
        came(copy, there)

    for at, ok, i, j in ((0, down, 0, 0), (33, up, 1, 2)):
        place(
            at,
            jnp.where(ok, hx[i].astype(F32), 0.0),
            jnp.where(ok & left, hc[j], 0.0),
            jnp.where(ok & right, hc[j + 1], 0.0),
        )
    low32 = lanes((32, 128)) < 64
    x32 = sublanes((32, 256))
    for i, ok in enumerate((left, right)):
        v = jnp.where(ok, hy[i].astype(F32), 0.0)
        lhs = jnp.concatenate(
            [
                jnp.concatenate([v[:, 0:256], jnp.where(low32, v[:, 256:384], 0.0)], axis=1),
                jnp.concatenate([v[:, 256:512], jnp.where(low32, 0.0, v[:, 128:256])], axis=1),
            ],
            axis=0,
        ).astype(BF)
        part = [
            jnp.dot(lhs, bw[0, 3 * dx + 2 * i], preferred_element_type=F32) for dx in range(3)
        ]
        for g in range(2):
            before, here, after = [p[g * 32 : (g + 1) * 32] for p in part]
            yl[i, g] = (
                here
                + jnp.where(x32 == 0, 0.0, pltpu.roll(before, 1, 0))
                + jnp.where(x32 == 31, 0.0, pltpu.roll(after, 31, 0))
            )
    for at, x, k in ((0, 0, 0), (33, 31, 6)):
        cacc[x] = cacc[x] + jnp.dot(
            cp[at].reshape(32, 1152),
            bw[0, k : k + 3].reshape(1152, 256),
            preferred_element_type=F32,
        ).reshape(2, 16, 256)
    y256 = sublanes((16, 256))

    def coarse_out(x, carry):
        for g in range(2):
            v = cacc[x, g]
            v = v + jnp.where(y256 == 0, yl[0, g, pl.ds(x, 1), :], 0.0)
            v = v + jnp.where(y256 == 15, yl[1, g, pl.ds(x, 1), :], 0.0)
            v = jnp.maximum(v, 0.0).astype(BF)
            cs[x, g] = v
            cout[x, :, g * 256 : (g + 1) * 256] = v
        return carry

    lax.fori_loop(0, X, coarse_out, 0, unroll=2)
    for m in range(0, nc, 4):
        psend[m : m + 4] = (
            jnp.dot(
                sel[m : m + 4].reshape(128, 1024),
                cs[...].reshape(1024, 256),
                preferred_element_type=F32,
            )
            .astype(BF)
            .reshape(4, 32, 256)
        )
        for k in range(m, m + 4):
            if k < nc - 1:
                remote(
                    psend.at[k], precv.at[c], gsem.at[0], gsem.at[1], (r, peers[k])
                ).start()
    gives = remote(
        psend.at[pl.ds(0, nc - 1)],
        precv.at[pl.ds(0, nc - 1)],
        gsem.at[0],
        gsem.at[1],
        (r, peers[0]),
    )
    precv[c] = psend[nc - 1]
    lw1.wait()
    build_weights(vw.at[1], bw.at[1])
    lw2.wait()
    build_weights(vw.at[2], bw.at[2])
    lfin.wait()
    lnb.wait()
    b8 = sublanes((8, 128))
    low = lanes((8, 128)) < 64
    index, local, cross = [], [], []
    for f in range(6):
        linked = jnp.full((8, 128), -1, jnp.int32)
        for b in range(NB):
            linked = jnp.where(b8 == b, nb[b, f], linked)
        owner = linked >> 3
        index.append(linked & 7)
        local.append(owner == me)
        other = me + (-nc, nc, -1, 1, -1, 1)[f]
        cross.append((linked >= 0) & (owner == other))

    base = jnp.zeros((8, 128), jnp.int32)
    for b in range(NB):
        base = jnp.where(b8 == b, tiles[b] * 32 + slots[b] * 16, base)
    l8 = lanes((8, 128))
    rows = []
    for q in range(16):
        rows.append(
            jnp.concatenate(
                [
                    jnp.where(base + q == l8 + k * 128, 1.0, 0.0)
                    for k in range(nc * 32 // 128)
                ],
                axis=1,
            )
        )
    sel2 = jnp.concatenate(rows, axis=0).astype(BF)

    zero8 = jnp.zeros((8, 128), F32)
    blank = jnp.zeros((16, 384), BF)
    for i in (0, 9):
        for j in (0, 9):
            pad[i, j] = blank
    in_local = [jnp.concatenate([m] * 4, axis=1) for m in local[:4]]
    in_cross = [jnp.concatenate([m] * 4, axis=1) for m in cross[:4]]
    for copy, there, _ in halos:
        sent(copy, there)
    gives.wait_recv()
    parents = jnp.dot(sel2, precv[...].reshape(nc * 32, 256), preferred_element_type=F32)
    grown = []
    for q in range(16):
        u = parents[q * 8 : (q + 1) * 8]
        parts = []
        for k in (0, 128):
            v = u[:, k : k + 128]
            w = pltpu.roll(v, 64, 1)
            parts += [jnp.where(low, v, w), jnp.where(low, w, v)]
        grown.append(jnp.concatenate(parts, axis=1))

    def begin(x, y):
        o = (x * 8 + y) * 512
        v = vf[:, o : o + 512].astype(F32) + grown[(x // 2) * 4 + y // 2]
        s1[x, y] = jnp.concatenate([v[:, 0:256], v[:, 256:512]], axis=0).astype(BF)

    def face(s, turn, f):
        src = s.at[7 if f == 0 else 0] if f < 2 else s.at[:, 7 if f == 2 else 0]
        to, frm = ((2, 3), (3, 2), (0, 1), (1, 0))[f]
        copy = remote(src, fr.at[turn, f], hsend.at[f], frecv.at[turn, f], near[to][0])
        start(copy, near[to][1])
        return copy, near[to][1], near[frm][1]

    inside = range(1, 7)
    for x in range(8):
        begin(x, 0)
        begin(x, 7)
    ymoves = [face(s1, 0, f) for f in (2, 3)]
    for y in inside:
        begin(0, y)
        begin(7, y)
    moves = [face(s1, 0, f) for f in (0, 1)] + ymoves
    for x in inside:
        for y in inside:
            begin(x, y)

    def fine_main(s, turn):
        def inner(x, carry):
            for y in range(8):
                v = load_cell(s, x, y)
                zm = jnp.where(local[4], take(v[:, 384:512], index[4]), 0.0)
                zp = jnp.where(local[5], take(v[:, 0:128], index[5]), 0.0)
                pad[x + 1, y + 1] = pack6(v, zm, zp, low)
            for f in range(4):
                k = 7 if f % 2 == 0 else 0
                v = load_cell(s, k, x) if f < 2 else load_cell(s, x, k)
                v = pack6(jnp.where(in_local[f], take(v, index[f]), 0.0), zero8, zero8, low)
                if f < 2:
                    pad[9 * f, x + 1] = v
                else:
                    pad[x + 1, 9 * (f - 2)] = v
            return carry

        lax.fori_loop(0, 8, inner, 0)
        bias = bt[turn + 1]

        def conv(i, carry):
            x0 = i * 4
            left = jnp.concatenate(
                [
                    pad[pl.ds(x0 + dx, 4), dy : dy + 8].reshape(512, 384)
                    for dx in range(3)
                    for dy in range(3)
                ],
                axis=1,
            )
            out = jnp.dot(left, bw[turn + 1].reshape(3456, 256), preferred_element_type=F32)
            facc[pl.ds(x0, 4)] = (out + bias).reshape(4, 8, 16, 256)
            return carry

        lax.fori_loop(0, 2, conv, 0)

    def fine_fix(turn, moves):
        for pair in ((0, 1), (2, 3)):
            for f in pair:
                came(moves[f][0], moves[f][2])
            adds = []
            for f in pair:
                tap = 2 * (f % 2)
                cells_of = [blank]
                for k in range(8):
                    v = load_cell(fr, turn, f, k)
                    v = jnp.where(in_cross[f], take(v, index[f]), 0.0)
                    cells_of.append(pack6(v, zero8, zero8, low))
                cells_of.append(blank)
                lhs = jnp.concatenate(
                    [jnp.concatenate(cells_of[d : d + 8], axis=0) for d in range(3)], axis=1
                )
                taps = [3 * tap + d if f < 2 else 3 * d + tap for d in range(3)]
                rhs = jnp.concatenate([bw[turn + 1, k] for k in taps], axis=0)
                adds.append(
                    jnp.dot(lhs, rhs, preferred_element_type=F32).reshape(8, 16, 256)
                )
            for f, add in zip(pair, adds):
                k = 7 * (f % 2)
                if f < 2:
                    facc[k] = facc[k] + add
                else:
                    facc[:, k] = facc[:, k] + add

    def keep(x, y):
        s2[x, y] = jnp.maximum(facc[x, y], 0.0).astype(BF)

    def final(x, y):
        v = jnp.maximum(facc[x, y], 0.0)
        at = pl.multiple_of((x * 8 + y) * 512, 512)
        fout[:, pl.ds(at, 512)] = jnp.concatenate([v[0:8], v[8:16]], axis=1).astype(BF)

    def each_inside(put):
        def one(x, carry):
            for y in inside:
                put(x, y)
            return carry

        lax.fori_loop(1, 7, one, 0)

    fine_main(s1, 0)
    each_inside(keep)
    fine_fix(0, moves)
    for x in range(8):
        keep(x, 0)
        keep(x, 7)
    for copy, there, _ in moves:
        sent(copy, there)
    ymoves = [face(s2, 1, f) for f in (2, 3)]
    for y in inside:
        keep(0, y)
        keep(7, y)
    moves = [face(s2, 1, f) for f in (0, 1)] + ymoves
    fine_main(s2, 1)
    each_inside(final)
    fine_fix(1, moves)
    for x in range(8):
        final(x, 0)
        final(x, 7)
    for y in inside:
        final(0, y)
        final(7, y)
    for copy, there, _ in moves:
        sent(copy, there)
    asks.wait_send()
    gives.wait_send()


def put_out(coarse, fine, coarse_hbm, fine_hbm, sem):
    copies = []
    for k in range(PARTS):
        n = X // PARTS
        x = slice(k * n, (k + 1) * n)
        copies.append(pltpu.make_async_copy(coarse.at[x], coarse_hbm.at[x], sem.at[2 * k]))
        n = 32768 // PARTS
        x = slice(k * n, (k + 1) * n)
        copies.append(
            pltpu.make_async_copy(fine.at[:, x], fine_hbm.at[:, x], sem.at[2 * k + 1])
        )
    for copy in copies:
        copy.start()
    for copy in copies:
        copy.wait()


def shards(
    coarse_in,
    coarse_weight,
    coarse_bias,
    fine_in,
    weight_first,
    bias_first,
    weight_second,
    bias_second,
    parent_tile,
    parent_cell,
    neighbours,
):
    nr = lax.axis_size("row")
    nc = lax.axis_size("col")
    anywhere = pl.BlockSpec(memory_space=pl.ANY)
    vector = pl.BlockSpec(memory_space=pltpu.VMEM)
    dma = pltpu.SemaphoreType.DMA
    coarse, fine = pl.pallas_call(
        functools.partial(body, nr, nc),
        out_shape=(pltpu.VMEM(coarse_in.shape, BF), pltpu.VMEM(fine_in.shape, BF)),
        in_specs=[anywhere] * 11,
        out_specs=(vector, vector),
        scratch_shapes=[
            pltpu.SMEM((NB,), jnp.int32),
            pltpu.SMEM((NB,), jnp.int32),
            pltpu.SMEM((NB, 6), jnp.int32),
            pltpu.VMEM((3, 1, CH), F32),
            pltpu.VMEM((X, Y, 512), BF),
            pltpu.VMEM((NB, 32768), BF),
            pltpu.VMEM((3, 27, CH, CH), BF),
            pltpu.VMEM((3, 9, 384, 256), BF),
            pltpu.VMEM((3, 1, 256), F32),
            pltpu.VMEM((64, 512), BF),
            pltpu.VMEM((4, 1, 512), F32),
            pltpu.VMEM((2, 16, 512), BF),
            pltpu.VMEM((2, 32, 512), BF),
            pltpu.VMEM((4, 1, 512), F32),
            pltpu.VMEM((2, 2, 32, 256), F32),
            pltpu.VMEM((34, 2, 16, 1152), BF),
            pltpu.VMEM((X, 2, 16, 256), F32),
            pltpu.VMEM((X, 2, 16, 256), BF),
            pltpu.VMEM((nc, 1, 128), jnp.int32),
            pltpu.VMEM((nc, 1, 128), jnp.int32),
            pltpu.VMEM((nc, 32, 1024), BF),
            pltpu.VMEM((nc, 32, 256), BF),
            pltpu.VMEM((nc, 32, 256), BF),
            pltpu.VMEM((8, 8, 16, 256), BF),
            pltpu.VMEM((8, 8, 16, 256), BF),
            pltpu.VMEM((2, 4, 8, 16, 256), BF),
            pltpu.VMEM((10, 10, 16, 384), BF),
            pltpu.VMEM((8, 8, 16, 256), F32),
            dma((11,)),
            dma((8,)),
            dma((8,)),
            dma((2,)),
            dma((2,)),
            dma((2, 4)),
        ],
        compiler_params=pltpu.CompilerParams(collective_id=0, has_side_effects=True),
    )(
        coarse_in,
        coarse_weight,
        coarse_bias.reshape(1, CH),
        fine_in,
        weight_first,
        bias_first.reshape(1, CH),
        weight_second,
        bias_second.reshape(1, CH),
        parent_tile.reshape(NB),
        parent_cell,
        neighbours,
    )
    return pl.pallas_call(
        put_out,
        out_shape=(
            jax.ShapeDtypeStruct(coarse_in.shape, BF),
            jax.ShapeDtypeStruct(fine_in.shape, BF),
        ),
        in_specs=[anywhere, anywhere],
        out_specs=(anywhere, anywhere),
        scratch_shapes=[dma((2 * PARTS,))],
        compiler_params=pltpu.CompilerParams(vmem_limit_bytes=1 << 20),
    )(coarse, fine)


def solution(mesh):
    placed = (
        P("row", "col", None),
        P(),
        P(),
        P(("row", "col"), None),
        P(),
        P(),
        P(),
        P(),
        P(("row", "col"), None),
        P(("row", "col")),
        P(("row", "col"), None),
    )
    return jax.shard_map(
        shards,
        mesh=mesh,
        in_specs=placed,
        out_specs=(P("row", "col", None), P(("row", "col"), None)),
        check_vma=False,
    )
```

```python
import functools
import jax
import jax.numpy as jnp
from jax import lax
from jax.experimental import pallas as pl
from jax.experimental.pallas import tpu as pltpu
from jax.sharding import PartitionSpec as P

CH = 64
X = 32
Y = 16
NB = 8
PARTS = 2
F32 = jnp.float32
BF = jnp.bfloat16
MESH = pl.DeviceIdType.MESH


def lanes(shape):
    return lax.broadcasted_iota(jnp.int32, shape, len(shape) - 1)


def sublanes(shape):
    return lax.broadcasted_iota(jnp.int32, shape, len(shape) - 2)


def build_weights(w, bw):
    zero = jnp.zeros((64, 64), BF)

    def one(k, carry):
        wm, w0, wp = w[3 * k], w[3 * k + 1], w[3 * k + 2]
        a = jnp.concatenate([w0, wm], axis=1)
        b = jnp.concatenate([wp, w0], axis=1)
        c = jnp.concatenate([zero, wp], axis=1)
        d = jnp.concatenate([wm, zero], axis=1)
        for r, v in enumerate((a, b, c)):
            bw[k, r * 64 : (r + 1) * 64, 0:128] = v
            bw[k, (r + 2) * 64 : (r + 3) * 64, 128:256] = v
        bw[k, 320:384, 0:128] = d
        bw[k, 64:128, 128:256] = d
        return carry

    lax.fori_loop(0, 9, one, 0, unroll=9)


def blank_weights(bw):
    wide = jnp.zeros((64, 128), BF)

    def one(k, carry):
        for i in range(3):
            for r, at in ((0, 128), (3, 0), (4, 0), (5, 128)):
                bw[i, k, r * 64 : (r + 1) * 64, at : at + 128] = wide
        return carry

    lax.fori_loop(0, 9, one, 0)


def parent_weights(w, cu):
    zero = jnp.zeros((64, 64), BF)
    wide = jnp.zeros((64, 128), BF)
    taps = {(0, 0): (0,), (0, 1): (1, 2), (1, 0): (0, 1), (1, 1): (2,)}
    xs = {}
    for key in taps:
        for k in range(9):
            xs[key, k] = sum(w[9 * d + k].astype(F32) for d in taps[key])
    for px, tx in taps:
        for py, ty in taps:
            t = [
                sum(xs[(px, tx), 3 * d + z] for d in taps[py, ty]) for z in range(3)
            ]
            a, b, d, e = [v.astype(BF) for v in (t[0], t[0] + t[1], t[1] + t[2], t[2])]
            one = jnp.concatenate([d, b], axis=1)
            two = jnp.concatenate([zero, e], axis=1)
            three = jnp.concatenate([a, zero], axis=1)
            for r, (left, right) in enumerate(
                ((one, three), (two, one), (wide, two), (three, wide))
            ):
                cu[px, py, tx, ty, r * 64 : (r + 1) * 64, 0:128] = left
                cu[px, py, tx, ty, r * 64 : (r + 1) * 64, 128:256] = right


def tile_bias(b, bt):
    for i in range(4):
        bt[:, i * 64 : (i + 1) * 64] = b[...]


def take(v, idx):
    return jnp.concatenate(
        [
            jnp.take_along_axis(v[:, k : k + 128], idx, axis=0, mode="promise_in_bounds")
            for k in range(0, v.shape[1], 128)
        ],
        axis=1,
    )


def pack6(v, zm, zp, low):
    first = jnp.concatenate([v[:, 0:256], jnp.where(low, v[:, 256:384], zm)], axis=1)
    second = jnp.concatenate([v[:, 256:512], jnp.where(low, zp, v[:, 128:256])], axis=1)
    return jnp.concatenate([first, second], axis=0).astype(BF)


def pack4(u, zm, zp, low):
    first = jnp.concatenate([u[:, 0:128], jnp.where(low, u[:, 128:256], zm)], axis=1)
    second = jnp.concatenate([u[:, 128:256], jnp.where(low, zp, u[:, 0:128])], axis=1)
    return jnp.concatenate([first, second], axis=0).astype(BF)


def load_cell(s, *at):
    v = s[at].astype(F32)
    return jnp.concatenate([v[0:8], v[8:16]], axis=1)


def order(nc):
    side = {16: 4, 4: 2}[nc]
    dist = lambda v: min(v, side - v)
    pairs = [(a, b) for a in range(side) for b in range(side)]
    return side, sorted(pairs, key=lambda p: -dist(p[0]) - dist(p[1]))


def body(
    nr,
    nc,
    cin,
    cw,
    cb,
    fin,
    w1,
    b1,
    w2,
    b2,
    ptile_in,
    pcell_in,
    nb_in,
    cout,
    fout,
    ptile,
    pcell,
    nb,
    braw,
    vin,
    vf,
    vw,
    bw,
    bt,
    edge,
    crn,
    hx,
    hy,
    hc,
    yl,
    cp,
    cacc,
    cs,
    req,
    reqr,
    sel,
    psend,
    precv,
    s1,
    s2,
    fr,
    pad,
    facc,
    cu,
    ub,
    fu,
    pu,
    lsem,
    hsend,
    hrecv,
    asem,
    gsem,
    fsend,
    frecv,
    urecv,
):
    r = lax.axis_index("row")
    c = lax.axis_index("col")
    me = r * nc + c
    side, offsets = order(nc)
    cy, cz = lax.div(c, side), lax.rem(c, side)
    peers = [lax.rem(cy + a, side) * side + lax.rem(cz + b, side) for a, b in offsets]
    up, down, right, left = r < nr - 1, r > 0, c < nc - 1, c > 0
    barrier = pltpu.get_barrier_semaphore()
    near = [
        ((r, c + 1), right),
        ((r, c - 1), left),
        ((r + 1, c), up),
        ((r - 1, c), down),
        ((r + 1, c + 1), up & right),
        ((r + 1, c - 1), up & left),
        ((r - 1, c + 1), down & right),
        ((r - 1, c - 1), down & left),
    ]
    heard = jnp.int32(nc - 1)
    for d in peers[:-1]:
        pl.semaphore_signal(barrier, inc=1, device_id=(r, d), device_id_type=MESH)
    for peer, there in near[2:]:
        heard = heard + jnp.where(there, 1, 0)

        @pl.when(there)
        def _(peer=peer):
            pl.semaphore_signal(barrier, inc=1, device_id=peer, device_id_type=MESH)

    loads = [
        pltpu.make_async_copy(cin, vin, lsem.at[0]),
        pltpu.make_async_copy(ptile_in, ptile, lsem.at[5]),
        pltpu.make_async_copy(pcell_in, pcell, lsem.at[6]),
        pltpu.make_async_copy(cw, vw.at[0], lsem.at[1]),
        pltpu.make_async_copy(nb_in, nb, lsem.at[7]),
        pltpu.make_async_copy(cb, braw.at[0], lsem.at[8]),
        pltpu.make_async_copy(b1, braw.at[1], lsem.at[9]),
        pltpu.make_async_copy(b2, braw.at[2], lsem.at[10]),
        pltpu.make_async_copy(fin, vf, lsem.at[2]),
        pltpu.make_async_copy(w1, vw.at[1], lsem.at[3]),
        pltpu.make_async_copy(w2, vw.at[2], lsem.at[4]),
    ]
    lin, ltile, lcell, lcw, lnb, lb0, lb1, lb2, lfin, lw1, lw2 = loads
    for copy in loads:
        copy.start()

    def remote(src, dst, ssem, rsem, peer):
        return pltpu.make_async_remote_copy(
            src_ref=src,
            dst_ref=dst,
            send_sem=ssem,
            recv_sem=rsem,
            device_id=peer,
            device_id_type=MESH,
        )

    def start(copy, there):
        @pl.when(there)
        def _():
            copy.start()

    def sent(copy, there):
        @pl.when(there)
        def _():
            copy.wait_send()

    def came(copy, there):
        @pl.when(there)
        def _():
            copy.wait_recv()
    ei = sublanes((64, 512))
    ej = lanes((64, 512))
    pick = jnp.where(ej == jnp.where(ei < 32, ei * 16 + 15, (ei - 32) * 16), 1.0, 0.0).astype(BF)
    blank_weights(bw)
    ltile.wait()
    lcell.wait()
    tiles = [ptile[b] for b in range(NB)]
    cells = [pcell[b] for b in range(NB)]
    slots = []
    for b in range(NB):
        n = jnp.int32(0)
        for e in range(b):
            n = n + jnp.where(tiles[e] == tiles[b], 1, 0)
        slots.append(n)
    row_id = sublanes((nc, 128))
    wanted = jnp.zeros((nc, 128), jnp.int32)
    for b in range(NB):
        ask = (cells[b] + 1) * jnp.where(slots[b] == 0, 1, 128)
        wanted = wanted + jnp.where(row_id == tiles[b], ask, 0)
    for t in range(nc):
        req[t] = wanted[t : t + 1]

    lin.wait()
    found = jnp.dot(pick, vin[...].reshape(512, 512), preferred_element_type=F32)
    edge[...] = found.astype(BF)
    for i, row in enumerate((31, 63, 0, 32)):
        crn[i] = found[row : row + 1]
    lcw.wait()
    build_weights(vw.at[0], bw.at[0])
    lb0.wait()
    lb1.wait()
    lb2.wait()
    for i in range(3):
        tile_bias(braw.at[i], bt.at[i])
    pl.semaphore_wait(barrier, heard)
    for d in peers[:-1]:
        remote(req.at[d], reqr.at[c], asem.at[0], asem.at[1], (r, d)).start()
    asks = remote(
        req.at[pl.ds(0, nc - 1)],
        reqr.at[pl.ds(0, nc - 1)],
        asem.at[0],
        asem.at[1],
        (r, peers[0]),
    )
    halos = []
    for i, (src, dst, to, frm) in enumerate(
        (
            (crn.at[0], hc.at[0], 4, 7),
            (crn.at[1], hc.at[1], 5, 6),
            (crn.at[2], hc.at[2], 6, 5),
            (crn.at[3], hc.at[3], 7, 4),
            (edge.at[0:32], hy.at[0], 0, 1),
            (edge.at[32:64], hy.at[1], 1, 0),
            (vin.at[31], hx.at[0], 2, 3),
            (vin.at[0], hx.at[1], 3, 2),
        )
    ):
        copy = remote(src, dst, hsend.at[i], hrecv.at[i], near[to][0])
        start(copy, near[to][1])
        halos.append((copy, near[to][1], near[frm][1]))
    reqr[c] = req[c]

    def face(s, last, dst, ssem, rsem, f):
        src = s.at[last if f == 0 else 0] if f < 2 else s.at[:, last if f == 2 else 0]
        to, frm = ((2, 3), (3, 2), (0, 1), (1, 0))[f]
        copy = remote(src, dst.at[f], ssem.at[f], rsem.at[f], near[to][0])
        start(copy, near[to][1])
        return copy, near[to][1], near[frm][1]

    def begin(x, y):
        o = (x * 8 + y) * 512
        v = vf[:, o : o + 512].astype(F32)
        s1[x, y] = jnp.concatenate([v[:, 0:256], v[:, 256:512]], axis=0).astype(BF)

    inside = range(1, 7)
    lfin.wait()
    for x in range(8):
        begin(x, 0)
        begin(x, 7)
    for y in inside:
        begin(0, y)
        begin(7, y)
    moves = [face(s1, 7, fr.at[0], fsend, frecv.at[0], f) for f in range(4)]

    low16 = lanes((16, 128)) < 64
    zero16 = jnp.zeros((16, 128), F32)
    y16 = sublanes((16, 512))

    def place(at, a, left, right):
        for dy, v in enumerate(
            (
                jnp.where(y16 == 0, left, pltpu.roll(a, 1, 0)),
                a,
                jnp.where(y16 == 15, right, pltpu.roll(a, 15, 0)),
            )
        ):
            o = dy * 384
            cp[at, 0, :, o : o + 256] = v[:, 0:256].astype(BF)
            cp[at, 0, :, o + 256 : o + 384] = jnp.where(low16, v[:, 256:384], zero16).astype(BF)
            cp[at, 1, :, o : o + 256] = v[:, 256:512].astype(BF)
            cp[at, 1, :, o + 256 : o + 384] = jnp.where(low16, zero16, v[:, 128:256]).astype(BF)

    def coarse_one(x, carry):
        place(x + 1, vin[x].astype(F32), 0.0, 0.0)
        return carry

    lax.fori_loop(0, X, coarse_one, 0)
    blank = jnp.zeros((2, 16, 1152), BF)
    cp[0] = blank
    cp[33] = blank
    cbias = bt[0]

    def coarse_conv(i, carry):
        x0 = i * 16
        left = jnp.concatenate(
            [cp[pl.ds(x0 + dx, 16)].reshape(512, 1152) for dx in range(3)], axis=1
        )
        out = jnp.dot(left, bw[0].reshape(3456, 256), preferred_element_type=F32)
        cacc[pl.ds(x0, 16)] = (out + cbias).reshape(16, 2, 16, 256)
        return carry

    lax.fori_loop(0, 2, coarse_conv, 0)
    for copy, _, there in halos:
        came(copy, there)

    for at, ok, i, j in ((0, down, 0, 0), (33, up, 1, 2)):
        place(
            at,
            jnp.where(ok, hx[i].astype(F32), 0.0),
            jnp.where(ok & left, hc[j], 0.0),
            jnp.where(ok & right, hc[j + 1], 0.0),
        )
    low32 = lanes((32, 128)) < 64
    x32 = sublanes((32, 256))
    for i, ok in enumerate((left, right)):
        v = jnp.where(ok, hy[i].astype(F32), 0.0)
        lhs = jnp.concatenate(
            [
                jnp.concatenate([v[:, 0:256], jnp.where(low32, v[:, 256:384], 0.0)], axis=1),
                jnp.concatenate([v[:, 256:512], jnp.where(low32, 0.0, v[:, 128:256])], axis=1),
            ],
            axis=0,
        ).astype(BF)
        part = [
            jnp.dot(lhs, bw[0, 3 * dx + 2 * i], preferred_element_type=F32) for dx in range(3)
        ]
        for g in range(2):
            before, here, after = [p[g * 32 : (g + 1) * 32] for p in part]
            yl[i, g] = (
                here
                + jnp.where(x32 == 0, 0.0, pltpu.roll(before, 1, 0))
                + jnp.where(x32 == 31, 0.0, pltpu.roll(after, 31, 0))
            )
    for at, x, k in ((0, 0, 0), (33, 31, 6)):
        cacc[x] = cacc[x] + jnp.dot(
            cp[at].reshape(32, 1152),
            bw[0, k : k + 3].reshape(1152, 256),
            preferred_element_type=F32,
        ).reshape(2, 16, 256)
    y256 = sublanes((16, 256))

    def coarse_out(x, carry):
        for g in range(2):
            v = cacc[x, g]
            v = v + jnp.where(y256 == 0, yl[0, g, pl.ds(x, 1), :], 0.0)
            v = v + jnp.where(y256 == 15, yl[1, g, pl.ds(x, 1), :], 0.0)
            v = jnp.maximum(v, 0.0).astype(BF)
            cs[x, g] = v
            cout[x, :, g * 256 : (g + 1) * 256] = v
        return carry

    lax.fori_loop(0, X, coarse_out, 0, unroll=2)

    asks.wait_recv()
    i16 = sublanes((16, 128))
    l16 = lanes((16, 128))
    def choose(k, d):
        both = jnp.broadcast_to(reqr[d], (16, 128))
        for s in range(2):
            cell = ((both >> (7 * s)) & 127) - 1
            px = (cell >> 3) * 4 + (i16 >> 2)
            py = ((cell >> 1) & 3) * 4 + (i16 & 3)
            target = jnp.where(cell >= 0, (px * 2 + (cell & 1)) * 16 + py, -1)
            for j in range(8):
                sel[k, s * 16 : (s + 1) * 16, j * 128 : (j + 1) * 128] = jnp.where(
                    target == l16 + j * 128, 1.0, 0.0
                ).astype(BF)
    for m in range(0, nc, 4):
        for k in range(m, m + 4):
            choose(k, peers[k])
        psend[m : m + 4] = (
            jnp.dot(
                sel[m : m + 4].reshape(128, 1024),
                cs[...].reshape(1024, 256),
                preferred_element_type=F32,
            )
            .astype(BF)
            .reshape(4, 32, 256)
        )
        for k in range(m, m + 4):
            if k < nc - 1:
                remote(
                    psend.at[k], precv.at[c], gsem.at[0], gsem.at[1], (r, peers[k])
                ).start()
    gives = remote(
        psend.at[pl.ds(0, nc - 1)],
        precv.at[pl.ds(0, nc - 1)],
        gsem.at[0],
        gsem.at[1],
        (r, peers[0]),
    )
    precv[c] = psend[nc - 1]
    lw1.wait()
    build_weights(vw.at[1], bw.at[1])
    lw2.wait()
    lnb.wait()
    b8 = sublanes((8, 128))
    low = lanes((8, 128)) < 64
    index, local, cross = [], [], []
    for f in range(6):
        linked = jnp.full((8, 128), -1, jnp.int32)
        for b in range(NB):
            linked = jnp.where(b8 == b, nb[b, f], linked)
        owner = linked >> 3
        index.append(linked & 7)
        local.append(owner == me)
        other = me + (-nc, nc, -1, 1, -1, 1)[f]
        cross.append((linked >= 0) & (owner == other))

    base = jnp.zeros((8, 128), jnp.int32)
    for b in range(NB):
        base = jnp.where(b8 == b, tiles[b] * 32 + slots[b] * 16, base)
    l8 = lanes((8, 128))
    rows = []
    for q in range(16):
        rows.append(
            jnp.concatenate(
                [
                    jnp.where(base + q == l8 + k * 128, 1.0, 0.0)
                    for k in range(nc * 32 // 128)
                ],
                axis=1,
            )
        )
    sel2 = jnp.concatenate(rows, axis=0).astype(BF)

    zero8 = jnp.zeros((8, 128), F32)
    blank = jnp.zeros((16, 384), BF)
    for i in (0, 9):
        for j in (0, 9):
            pad[i, j] = blank
    in_local = [jnp.concatenate([m] * 4, axis=1) for m in local[:4]]
    in_cross = [jnp.concatenate([m] * 4, axis=1) for m in cross[:4]]
    for copy, there, _ in halos:
        sent(copy, there)

    def fine_main(s, turn):
        def inner(x, carry):
            for y in range(8):
                v = load_cell(s, x, y)
                zm = jnp.where(local[4], take(v[:, 384:512], index[4]), 0.0)
                zp = jnp.where(local[5], take(v[:, 0:128], index[5]), 0.0)
                pad[x + 1, y + 1] = pack6(v, zm, zp, low)
            for f in range(4):
                k = 7 if f % 2 == 0 else 0
                v = load_cell(s, k, x) if f < 2 else load_cell(s, x, k)
                v = pack6(jnp.where(in_local[f], take(v, index[f]), 0.0), zero8, zero8, low)
                if f < 2:
                    pad[9 * f, x + 1] = v
                else:
                    pad[x + 1, 9 * (f - 2)] = v
            return carry

        lax.fori_loop(0, 8, inner, 0)
        bias = bt[turn + 1]

        def conv(i, carry):
            x0 = i * 4
            left = jnp.concatenate(
                [
                    pad[pl.ds(x0 + dx, 4), dy : dy + 8].reshape(512, 384)
                    for dx in range(3)
                    for dy in range(3)
                ],
                axis=1,
            )
            out = jnp.dot(left, bw[turn + 1].reshape(3456, 256), preferred_element_type=F32)
            facc[pl.ds(i * 2, 2)] = (out + bias).reshape(2, 2, 4, 2, 16, 256)
            return carry

        lax.fori_loop(0, 2, conv, 0)

    def fine_fix(turn, moves):
        for pair in ((0, 1), (2, 3)):
            for f in pair:
                came(moves[f][0], moves[f][2])
            adds = []
            for f in pair:
                tap = 2 * (f % 2)
                cells_of = [blank]
                for k in range(8):
                    v = load_cell(fr, turn, f, k)
                    v = jnp.where(in_cross[f], take(v, index[f]), 0.0)
                    cells_of.append(pack6(v, zero8, zero8, low))
                cells_of.append(blank)
                lhs = jnp.concatenate(
                    [jnp.concatenate(cells_of[d : d + 8], axis=0) for d in range(3)], axis=1
                )
                taps = [3 * tap + d if f < 2 else 3 * d + tap for d in range(3)]
                rhs = jnp.concatenate([bw[turn + 1, k] for k in taps], axis=0)
                adds.append(
                    jnp.dot(lhs, rhs, preferred_element_type=F32).reshape(8, 16, 256)
                )
            for f, add in zip(pair, adds):
                k, h = 3 * (f % 2), f % 2
                if f < 2:
                    facc[k, h] = facc[k, h] + add.reshape(4, 2, 16, 256)
                else:
                    facc[:, :, k, h] = facc[:, :, k, h] + add.reshape(4, 2, 16, 256)

    def add_to(x, y):
        return facc[x // 2, x % 2, y // 2, y % 2]

    def keep(x, y):
        s2[x, y] = jnp.maximum(add_to(x, y), 0.0).astype(BF)

    def final(x, y):
        v = jnp.maximum(add_to(x, y), 0.0)
        fout[:, (x * 8 + y) * 512 : (x * 8 + y + 1) * 512] = jnp.concatenate(
            [v[0:8], v[8:16]], axis=1
        ).astype(BF)

    for x in inside:
        for y in inside:
            begin(x, y)
    fine_main(s1, 0)
    parent_weights(vw.at[1], cu)
    fine_fix(0, moves)
    gives.wait_recv()
    parents = jnp.dot(sel2, precv[...].reshape(nc * 32, 256), preferred_element_type=F32)
    grown = [parents[q * 8 : (q + 1) * 8] for q in range(16)]
    for q in range(16):
        u = grown[q]
        ub[q // 4, q % 4] = jnp.concatenate([u[:, 0:128], u[:, 128:256]], axis=0).astype(BF)
    umoves = [face(ub, 3, fu, hsend, urecv, f) for f in range(4)]

    for q in range(16):
        u = grown[q]
        zm = jnp.where(local[4], take(u[:, 128:256], index[4]), 0.0)
        zp = jnp.where(local[5], take(u[:, 0:128], index[5]), 0.0)
        pu[q // 4 + 1, q % 4 + 1] = pack4(u, zm, zp, low)
    ublank = jnp.zeros((16, 256), BF)
    for i in (0, 5):
        for j in (0, 5):
            pu[i, j] = ublank
    for k in range(4):
        for f in range(4):
            at = 3 * (1 - f % 2)
            u = grown[at * 4 + k] if f < 2 else grown[k * 4 + at]
            half = in_local[f][:, 0:256]
            v = pack4(jnp.where(half, take(u, index[f]), 0.0), zero8, zero8, low)
            if f < 2:
                pu[5 * f, k + 1] = v
            else:
                pu[k + 1, 5 * (f - 2)] = v
    for px in range(2):
        for py in range(2):
            lhs = jnp.concatenate(
                [
                    pu[px + tx : px + tx + 4, py + ty : py + ty + 4].reshape(256, 256)
                    for tx in range(2)
                    for ty in range(2)
                ],
                axis=1,
            )
            out = jnp.dot(lhs, cu[px, py].reshape(1024, 256), preferred_element_type=F32)
            facc[:, px, :, py] = facc[:, px, :, py] + out.reshape(4, 4, 16, 256)
    build_weights(vw.at[2], bw.at[2])
    for pair in ((0, 1), (2, 3)):
        for f in pair:
            came(umoves[f][0], umoves[f][2])
        adds = []
        for f in pair:
            tap = f % 2
            strip = [ublank]
            for k in range(4):
                v = fu[f, k].astype(F32)
                u = jnp.concatenate([v[0:8], v[8:16]], axis=1)
                u = jnp.where(in_cross[f][:, 0:256], take(u, index[f]), 0.0)
                strip.append(pack4(u, zero8, zero8, low))
            strip.append(ublank)
            for p in range(2):
                lhs = jnp.concatenate(
                    [jnp.concatenate(strip[p + t : p + t + 4], axis=0) for t in range(2)],
                    axis=1,
                )
                if f < 2:
                    rhs = cu[tap, p, tap].reshape(512, 256)
                else:
                    rhs = jnp.concatenate([cu[p, tap, t, tap] for t in range(2)], axis=0)
                add = jnp.dot(lhs, rhs, preferred_element_type=F32).reshape(4, 16, 256)
                adds.append((f, p, add))
        for f, p, add in adds:
            e, tap = 3 * (f % 2), f % 2
            if f < 2:
                facc[e, tap, :, p] = facc[e, tap, :, p] + add
            else:
                facc[:, p, e, tap] = facc[:, p, e, tap] + add
    for x in range(8):
        keep(x, 0)
        keep(x, 7)
    for y in inside:
        keep(0, y)
        keep(7, y)
    for copy, there, _ in moves:
        sent(copy, there)
    moves = [face(s2, 7, fr.at[1], fsend, frecv.at[1], f) for f in (2, 3, 0, 1)]
    moves = moves[2:] + moves[:2]
    for x in inside:
        for y in inside:
            keep(x, y)
    fine_main(s2, 1)
    for x in inside:
        for y in inside:
            final(x, y)
    fine_fix(1, moves)
    for x in range(8):
        final(x, 0)
        final(x, 7)
    for y in inside:
        final(0, y)
        final(7, y)
    for copy, there, _ in moves + umoves:
        sent(copy, there)
    asks.wait_send()
    gives.wait_send()


def put_out(coarse, fine, coarse_hbm, fine_hbm, sem):
    copies = []
    for k in range(PARTS):
        n = X // PARTS
        x = slice(k * n, (k + 1) * n)
        copies.append(pltpu.make_async_copy(coarse.at[x], coarse_hbm.at[x], sem.at[2 * k]))
        n = 32768 // PARTS
        x = slice(k * n, (k + 1) * n)
        copies.append(
            pltpu.make_async_copy(fine.at[:, x], fine_hbm.at[:, x], sem.at[2 * k + 1])
        )
    for copy in copies:
        copy.start()
    for copy in copies:
        copy.wait()


def shards(
    coarse_in,
    coarse_weight,
    coarse_bias,
    fine_in,
    weight_first,
    bias_first,
    weight_second,
    bias_second,
    parent_tile,
    parent_cell,
    neighbours,
):
    nr = lax.axis_size("row")
    nc = lax.axis_size("col")
    anywhere = pl.BlockSpec(memory_space=pl.ANY)
    vector = pl.BlockSpec(memory_space=pltpu.VMEM)
    dma = pltpu.SemaphoreType.DMA
    coarse, fine = pl.pallas_call(
        functools.partial(body, nr, nc),
        out_shape=(pltpu.VMEM(coarse_in.shape, BF), pltpu.VMEM(fine_in.shape, BF)),
        in_specs=[anywhere] * 11,
        out_specs=(vector, vector),
        scratch_shapes=[
            pltpu.SMEM((NB,), jnp.int32),
            pltpu.SMEM((NB,), jnp.int32),
            pltpu.SMEM((NB, 6), jnp.int32),
            pltpu.VMEM((3, 1, CH), F32),
            pltpu.VMEM((X, Y, 512), BF),
            pltpu.VMEM((NB, 32768), BF),
            pltpu.VMEM((3, 27, CH, CH), BF),
            pltpu.VMEM((3, 9, 384, 256), BF),
            pltpu.VMEM((3, 1, 256), F32),
            pltpu.VMEM((64, 512), BF),
            pltpu.VMEM((4, 1, 512), F32),
            pltpu.VMEM((2, 16, 512), BF),
            pltpu.VMEM((2, 32, 512), BF),
            pltpu.VMEM((4, 1, 512), F32),
            pltpu.VMEM((2, 2, 32, 256), F32),
            pltpu.VMEM((34, 2, 16, 1152), BF),
            pltpu.VMEM((X, 2, 16, 256), F32),
            pltpu.VMEM((X, 2, 16, 256), BF),
            pltpu.VMEM((nc, 1, 128), jnp.int32),
            pltpu.VMEM((nc, 1, 128), jnp.int32),
            pltpu.VMEM((nc, 32, 1024), BF),
            pltpu.VMEM((nc, 32, 256), BF),
            pltpu.VMEM((nc, 32, 256), BF),
            pltpu.VMEM((8, 8, 16, 256), BF),
            pltpu.VMEM((8, 8, 16, 256), BF),
            pltpu.VMEM((2, 4, 8, 16, 256), BF),
            pltpu.VMEM((10, 10, 16, 384), BF),
            pltpu.VMEM((4, 2, 4, 2, 16, 256), F32),
            pltpu.VMEM((2, 2, 2, 2, 256, 256), BF),
            pltpu.VMEM((4, 4, 16, 128), BF),
            pltpu.VMEM((4, 4, 16, 128), BF),
            pltpu.VMEM((6, 6, 16, 256), BF),
            dma((11,)),
            dma((8,)),
            dma((8,)),
            dma((2,)),
            dma((2,)),
            dma((4,)),
            dma((2, 4)),
            dma((4,)),
        ],
        compiler_params=pltpu.CompilerParams(collective_id=0, has_side_effects=True),
    )(
        coarse_in,
        coarse_weight,
        coarse_bias.reshape(1, CH),
        fine_in,
        weight_first,
        bias_first.reshape(1, CH),
        weight_second,
        bias_second.reshape(1, CH),
        parent_tile.reshape(NB),
        parent_cell,
        neighbours,
    )
    return pl.pallas_call(
        put_out,
        out_shape=(
            jax.ShapeDtypeStruct(coarse_in.shape, BF),
            jax.ShapeDtypeStruct(fine_in.shape, BF),
        ),
        in_specs=[anywhere, anywhere],
        out_specs=(anywhere, anywhere),
        scratch_shapes=[dma((2 * PARTS,))],
        compiler_params=pltpu.CompilerParams(vmem_limit_bytes=1 << 20),
    )(coarse, fine)


def solution(mesh):
    placed = (
        P("row", "col", None),
        P(),
        P(),
        P(("row", "col"), None),
        P(),
        P(),
        P(),
        P(),
        P(("row", "col"), None),
        P(("row", "col")),
        P(("row", "col"), None),
    )
    return jax.shard_map(
        shards,
        mesh=mesh,
        in_specs=placed,
        out_specs=(P("row", "col", None), P(("row", "col"), None)),
        check_vma=False,
    )
```

```python
import functools
import jax
import jax.numpy as jnp
from jax import lax
from jax.experimental import pallas as pl
from jax.experimental.pallas import tpu as pltpu
from jax.sharding import PartitionSpec as P

CH = 64
X = 32
Y = 16
NB = 8
PARTS = 2
F32 = jnp.float32
BF = jnp.bfloat16
MESH = pl.DeviceIdType.MESH


def lanes(shape):
    return lax.broadcasted_iota(jnp.int32, shape, len(shape) - 1)


def sublanes(shape):
    return lax.broadcasted_iota(jnp.int32, shape, len(shape) - 2)


def build_weights(w, bw):
    zero = jnp.zeros((64, 64), BF)

    def one(k, carry):
        wm, w0, wp = w[3 * k], w[3 * k + 1], w[3 * k + 2]
        a = jnp.concatenate([w0, wm], axis=1)
        b = jnp.concatenate([wp, w0], axis=1)
        c = jnp.concatenate([zero, wp], axis=1)
        d = jnp.concatenate([wm, zero], axis=1)
        for r, v in enumerate((a, b, c)):
            bw[k, r * 64 : (r + 1) * 64, 0:128] = v
            bw[k, (r + 2) * 64 : (r + 3) * 64, 128:256] = v
        bw[k, 320:384, 0:128] = d
        bw[k, 64:128, 128:256] = d
        return carry

    lax.fori_loop(0, 9, one, 0, unroll=9)


def blank_weights(bw):
    wide = jnp.zeros((64, 128), BF)

    def one(k, carry):
        for i in range(3):
            for r, at in ((0, 128), (3, 0), (4, 0), (5, 128)):
                bw[i, k, r * 64 : (r + 1) * 64, at : at + 128] = wide
        return carry

    lax.fori_loop(0, 9, one, 0)


def parent_weights(w, cu):
    zero = jnp.zeros((64, 64), BF)
    wide = jnp.zeros((64, 128), BF)
    taps = {(0, 0): (0,), (0, 1): (1, 2), (1, 0): (0, 1), (1, 1): (2,)}
    xs = {}
    for key in taps:
        for k in range(9):
            xs[key, k] = sum(w[9 * d + k].astype(F32) for d in taps[key])
    for px, tx in taps:
        for py, ty in taps:
            t = [
                sum(xs[(px, tx), 3 * d + z] for d in taps[py, ty]) for z in range(3)
            ]
            a, b, d, e = [v.astype(BF) for v in (t[0], t[0] + t[1], t[1] + t[2], t[2])]
            one = jnp.concatenate([d, b], axis=1)
            two = jnp.concatenate([zero, e], axis=1)
            three = jnp.concatenate([a, zero], axis=1)
            for r, (left, right) in enumerate(
                ((one, three), (two, one), (wide, two), (three, wide))
            ):
                cu[px, py, tx, ty, r * 64 : (r + 1) * 64, 0:128] = left
                cu[px, py, tx, ty, r * 64 : (r + 1) * 64, 128:256] = right


def tile_bias(b, bt):
    for i in range(4):
        bt[:, i * 64 : (i + 1) * 64] = b[...]


def take(v, idx):
    return jnp.concatenate(
        [
            jnp.take_along_axis(v[:, k : k + 128], idx, axis=0, mode="promise_in_bounds")
            for k in range(0, v.shape[1], 128)
        ],
        axis=1,
    )


def pack6(v, zm, zp, low):
    first = jnp.concatenate([v[:, 0:256], jnp.where(low, v[:, 256:384], zm)], axis=1)
    second = jnp.concatenate([v[:, 256:512], jnp.where(low, zp, v[:, 128:256])], axis=1)
    return jnp.concatenate([first, second], axis=0).astype(BF)


def pack4(u, zm, zp, low):
    first = jnp.concatenate([u[:, 0:128], jnp.where(low, u[:, 128:256], zm)], axis=1)
    second = jnp.concatenate([u[:, 128:256], jnp.where(low, zp, u[:, 0:128])], axis=1)
    return jnp.concatenate([first, second], axis=0).astype(BF)


def load_cell(s, *at):
    v = s[at].astype(F32)
    return jnp.concatenate([v[0:8], v[8:16]], axis=1)


def order(nc):
    side = {16: 4, 4: 2}[nc]
    dist = lambda v: min(v, side - v)
    pairs = [(a, b) for a in range(side) for b in range(side)]
    return side, sorted(pairs, key=lambda p: -dist(p[0]) - dist(p[1]))


def body(
    nr,
    nc,
    cin,
    cw,
    cb,
    fin,
    w1,
    b1,
    w2,
    b2,
    ptile_in,
    pcell_in,
    nb_in,
    cout,
    fout,
    ptile,
    pcell,
    nb,
    braw,
    vin,
    vf,
    vw,
    bw,
    bt,
    edge,
    crn,
    hx,
    hy,
    hc,
    yl,
    cp,
    cacc,
    cs,
    req,
    reqr,
    sel,
    psend,
    precv,
    s1,
    s2,
    fr,
    pad,
    facc,
    cu,
    ub,
    fu,
    pu,
    lsem,
    hsend,
    hrecv,
    asem,
    gsem,
    fsend,
    frecv,
    urecv,
):
    r = lax.axis_index("row")
    c = lax.axis_index("col")
    me = r * nc + c
    side, offsets = order(nc)
    cy, cz = lax.div(c, side), lax.rem(c, side)
    peers = [lax.rem(cy + a, side) * side + lax.rem(cz + b, side) for a, b in offsets]
    up, down, right, left = r < nr - 1, r > 0, c < nc - 1, c > 0
    barrier = pltpu.get_barrier_semaphore()
    near = [
        ((r, c + 1), right),
        ((r, c - 1), left),
        ((r + 1, c), up),
        ((r - 1, c), down),
        ((r + 1, c + 1), up & right),
        ((r + 1, c - 1), up & left),
        ((r - 1, c + 1), down & right),
        ((r - 1, c - 1), down & left),
    ]
    heard = jnp.int32(nc - 1)
    for d in peers[:-1]:
        pl.semaphore_signal(barrier, inc=1, device_id=(r, d), device_id_type=MESH)
    for peer, there in near[2:]:
        heard = heard + jnp.where(there, 1, 0)

        @pl.when(there)
        def _(peer=peer):
            pl.semaphore_signal(barrier, inc=1, device_id=peer, device_id_type=MESH)

    loads = [
        pltpu.make_async_copy(cin, vin, lsem.at[0]),
        pltpu.make_async_copy(ptile_in, ptile, lsem.at[5]),
        pltpu.make_async_copy(pcell_in, pcell, lsem.at[6]),
        pltpu.make_async_copy(cw, vw.at[0], lsem.at[1]),
        pltpu.make_async_copy(nb_in, nb, lsem.at[7]),
        pltpu.make_async_copy(cb, braw.at[0], lsem.at[8]),
        pltpu.make_async_copy(b1, braw.at[1], lsem.at[9]),
        pltpu.make_async_copy(b2, braw.at[2], lsem.at[10]),
        pltpu.make_async_copy(fin, vf, lsem.at[2]),
        pltpu.make_async_copy(w1, vw.at[1], lsem.at[3]),
        pltpu.make_async_copy(w2, vw.at[2], lsem.at[4]),
    ]
    lin, ltile, lcell, lcw, lnb, lb0, lb1, lb2, lfin, lw1, lw2 = loads
    for copy in loads:
        copy.start()

    def remote(src, dst, ssem, rsem, peer):
        return pltpu.make_async_remote_copy(
            src_ref=src,
            dst_ref=dst,
            send_sem=ssem,
            recv_sem=rsem,
            device_id=peer,
            device_id_type=MESH,
        )

    def start(copy, there):
        @pl.when(there)
        def _():
            copy.start()

    def sent(copy, there):
        @pl.when(there)
        def _():
            copy.wait_send()

    def came(copy, there):
        @pl.when(there)
        def _():
            copy.wait_recv()
    ei = sublanes((64, 512))
    ej = lanes((64, 512))
    pick = jnp.where(ej == jnp.where(ei < 32, ei * 16 + 15, (ei - 32) * 16), 1.0, 0.0).astype(BF)
    blank_weights(bw)
    ltile.wait()
    lcell.wait()
    tiles = [ptile[b] for b in range(NB)]
    cells = [pcell[b] for b in range(NB)]
    slots = []
    for b in range(NB):
        n = jnp.int32(0)
        for e in range(b):
            n = n + jnp.where(tiles[e] == tiles[b], 1, 0)
        slots.append(n)
    row_id = sublanes((nc, 128))
    wanted = jnp.zeros((nc, 128), jnp.int32)
    for b in range(NB):
        ask = (cells[b] + 1) * jnp.where(slots[b] == 0, 1, 128)
        wanted = wanted + jnp.where(row_id == tiles[b], ask, 0)
    for t in range(nc):
        req[t] = wanted[t : t + 1]

    lin.wait()
    found = jnp.dot(pick, vin[...].reshape(512, 512), preferred_element_type=F32)
    edge[...] = found.astype(BF)
    for i, row in enumerate((31, 63, 0, 32)):
        crn[i] = found[row : row + 1]
    lcw.wait()
    build_weights(vw.at[0], bw.at[0])
    lb0.wait()
    lb1.wait()
    lb2.wait()
    for i in range(3):
        tile_bias(braw.at[i], bt.at[i])
    pl.semaphore_wait(barrier, heard)
    for d in peers[:-1]:
        remote(req.at[d], reqr.at[c], asem.at[0], asem.at[1], (r, d)).start()
    asks = remote(
        req.at[pl.ds(0, nc - 1)],
        reqr.at[pl.ds(0, nc - 1)],
        asem.at[0],
        asem.at[1],
        (r, peers[0]),
    )
    halos = []
    for i, (src, dst, to, frm) in enumerate(
        (
            (crn.at[0], hc.at[0], 4, 7),
            (crn.at[1], hc.at[1], 5, 6),
            (crn.at[2], hc.at[2], 6, 5),
            (crn.at[3], hc.at[3], 7, 4),
            (edge.at[0:32], hy.at[0], 0, 1),
            (edge.at[32:64], hy.at[1], 1, 0),
            (vin.at[31], hx.at[0], 2, 3),
            (vin.at[0], hx.at[1], 3, 2),
        )
    ):
        copy = remote(src, dst, hsend.at[i], hrecv.at[i], near[to][0])
        start(copy, near[to][1])
        halos.append((copy, near[to][1], near[frm][1]))
    reqr[c] = req[c]

    def face(s, last, dst, ssem, rsem, f):
        src = s.at[last if f == 0 else 0] if f < 2 else s.at[:, last if f == 2 else 0]
        to, frm = ((2, 3), (3, 2), (0, 1), (1, 0))[f]
        copy = remote(src, dst.at[f], ssem.at[f], rsem.at[f], near[to][0])
        start(copy, near[to][1])
        return copy, near[to][1], near[frm][1]

    def begin(x, y):
        o = (x * 8 + y) * 512
        v = vf[:, o : o + 512].astype(F32)
        s1[x, y] = jnp.concatenate([v[:, 0:256], v[:, 256:512]], axis=0).astype(BF)

    inside = range(1, 7)
    lfin.wait()
    for x in range(8):
        begin(x, 0)
        begin(x, 7)
    for y in inside:
        begin(0, y)
        begin(7, y)
    moves = [face(s1, 7, fr.at[0], fsend, frecv.at[0], f) for f in range(4)]

    low16 = lanes((16, 128)) < 64
    zero16 = jnp.zeros((16, 128), F32)
    y16 = sublanes((16, 512))

    def place(at, a, left, right):
        for dy, v in enumerate(
            (
                jnp.where(y16 == 0, left, pltpu.roll(a, 1, 0)),
                a,
                jnp.where(y16 == 15, right, pltpu.roll(a, 15, 0)),
            )
        ):
            o = dy * 384
            cp[at, 0, :, o : o + 256] = v[:, 0:256].astype(BF)
            cp[at, 0, :, o + 256 : o + 384] = jnp.where(low16, v[:, 256:384], zero16).astype(BF)
            cp[at, 1, :, o : o + 256] = v[:, 256:512].astype(BF)
            cp[at, 1, :, o + 256 : o + 384] = jnp.where(low16, zero16, v[:, 128:256]).astype(BF)

    def coarse_one(x, carry):
        place(x + 1, vin[x].astype(F32), 0.0, 0.0)
        return carry

    lax.fori_loop(0, X, coarse_one, 0)
    blank = jnp.zeros((2, 16, 1152), BF)
    cp[0] = blank
    cp[33] = blank
    cbias = bt[0]

    def coarse_conv(i, carry):
        x0 = i * 16
        left = jnp.concatenate(
            [cp[pl.ds(x0 + dx, 16)].reshape(512, 1152) for dx in range(3)], axis=1
        )
        out = jnp.dot(left, bw[0].reshape(3456, 256), preferred_element_type=F32)
        cacc[pl.ds(x0, 16)] = (out + cbias).reshape(16, 2, 16, 256)
        return carry

    lax.fori_loop(0, 2, coarse_conv, 0)
    for copy, _, there in halos:
        came(copy, there)

    for at, ok, i, j in ((0, down, 0, 0), (33, up, 1, 2)):
        place(
            at,
            jnp.where(ok, hx[i].astype(F32), 0.0),
            jnp.where(ok & left, hc[j], 0.0),
            jnp.where(ok & right, hc[j + 1], 0.0),
        )
    low32 = lanes((32, 128)) < 64
    x32 = sublanes((32, 256))
    for i, ok in enumerate((left, right)):
        v = jnp.where(ok, hy[i].astype(F32), 0.0)
        lhs = jnp.concatenate(
            [
                jnp.concatenate([v[:, 0:256], jnp.where(low32, v[:, 256:384], 0.0)], axis=1),
                jnp.concatenate([v[:, 256:512], jnp.where(low32, 0.0, v[:, 128:256])], axis=1),
            ],
            axis=0,
        ).astype(BF)
        part = [
            jnp.dot(lhs, bw[0, 3 * dx + 2 * i], preferred_element_type=F32) for dx in range(3)
        ]
        for g in range(2):
            before, here, after = [p[g * 32 : (g + 1) * 32] for p in part]
            yl[i, g] = (
                here
                + jnp.where(x32 == 0, 0.0, pltpu.roll(before, 1, 0))
                + jnp.where(x32 == 31, 0.0, pltpu.roll(after, 31, 0))
            )
    for at, x, k in ((0, 0, 0), (33, 31, 6)):
        cacc[x] = cacc[x] + jnp.dot(
            cp[at].reshape(32, 1152),
            bw[0, k : k + 3].reshape(1152, 256),
            preferred_element_type=F32,
        ).reshape(2, 16, 256)
    y256 = sublanes((16, 256))

    def coarse_out(x, carry):
        for g in range(2):
            v = cacc[x, g]
            v = v + jnp.where(y256 == 0, yl[0, g, pl.ds(x, 1), :], 0.0)
            v = v + jnp.where(y256 == 15, yl[1, g, pl.ds(x, 1), :], 0.0)
            v = jnp.maximum(v, 0.0).astype(BF)
            cs[x, g] = v
            cout[x, :, g * 256 : (g + 1) * 256] = v
        return carry

    lax.fori_loop(0, X, coarse_out, 0, unroll=2)

    asks.wait_recv()
    i16 = sublanes((16, 128))
    l16 = lanes((16, 128))
    def choose(k, d):
        both = jnp.broadcast_to(reqr[d], (16, 128))
        for s in range(2):
            cell = ((both >> (7 * s)) & 127) - 1
            px = (cell >> 3) * 4 + (i16 >> 2)
            py = ((cell >> 1) & 3) * 4 + (i16 & 3)
            target = jnp.where(cell >= 0, (px * 2 + (cell & 1)) * 16 + py, -1)
            for j in range(8):
                sel[k, s * 16 : (s + 1) * 16, j * 128 : (j + 1) * 128] = jnp.where(
                    target == l16 + j * 128, 1.0, 0.0
                ).astype(BF)
    for m in range(0, nc, 4):
        for k in range(m, m + 4):
            choose(k, peers[k])
        psend[m : m + 4] = (
            jnp.dot(
                sel[m : m + 4].reshape(128, 1024),
                cs[...].reshape(1024, 256),
                preferred_element_type=F32,
            )
            .astype(BF)
            .reshape(4, 32, 256)
        )
        for k in range(m, m + 4):
            if k < nc - 1:
                remote(
                    psend.at[k], precv.at[c], gsem.at[0], gsem.at[1], (r, peers[k])
                ).start()
    gives = remote(
        psend.at[pl.ds(0, nc - 1)],
        precv.at[pl.ds(0, nc - 1)],
        gsem.at[0],
        gsem.at[1],
        (r, peers[0]),
    )
    precv[c] = psend[nc - 1]
    lw1.wait()
    build_weights(vw.at[1], bw.at[1])
    lw2.wait()
    lnb.wait()
    b8 = sublanes((8, 128))
    low = lanes((8, 128)) < 64
    index, local, cross = [], [], []
    for f in range(6):
        linked = jnp.full((8, 128), -1, jnp.int32)
        for b in range(NB):
            linked = jnp.where(b8 == b, nb[b, f], linked)
        owner = linked >> 3
        index.append(linked & 7)
        local.append(owner == me)
        other = me + (-nc, nc, -1, 1, -1, 1)[f]
        cross.append((linked >= 0) & (owner == other))

    base = jnp.zeros((8, 128), jnp.int32)
    for b in range(NB):
        base = jnp.where(b8 == b, tiles[b] * 32 + slots[b] * 16, base)
    l8 = lanes((8, 128))
    rows = []
    for q in range(16):
        rows.append(
            jnp.concatenate(
                [
                    jnp.where(base + q == l8 + k * 128, 1.0, 0.0)
                    for k in range(nc * 32 // 128)
                ],
                axis=1,
            )
        )
    sel2 = jnp.concatenate(rows, axis=0).astype(BF)

    zero8 = jnp.zeros((8, 128), F32)
    blank = jnp.zeros((16, 384), BF)
    for i in (0, 9):
        for j in (0, 9):
            pad[i, j] = blank
    in_local = [jnp.concatenate([m] * 4, axis=1) for m in local[:4]]
    in_cross = [jnp.concatenate([m] * 4, axis=1) for m in cross[:4]]
    for copy, there, _ in halos:
        sent(copy, there)

    def by_parity(one):
        @pl.when(lax.rem(r, 2) == 0)
        def _():
            one((0, 1))

        one((2, 3))

        @pl.when(lax.rem(r, 2) == 1)
        def _():
            one((0, 1))

    def fine_main(s, turn):
        def inner(x, carry):
            for y in range(8):
                v = load_cell(s, x, y)
                zm = jnp.where(local[4], take(v[:, 384:512], index[4]), 0.0)
                zp = jnp.where(local[5], take(v[:, 0:128], index[5]), 0.0)
                pad[x + 1, y + 1] = pack6(v, zm, zp, low)
            for f in range(4):
                k = 7 if f % 2 == 0 else 0
                v = load_cell(s, k, x) if f < 2 else load_cell(s, x, k)
                v = pack6(jnp.where(in_local[f], take(v, index[f]), 0.0), zero8, zero8, low)
                if f < 2:
                    pad[9 * f, x + 1] = v
                else:
                    pad[x + 1, 9 * (f - 2)] = v
            return carry

        lax.fori_loop(0, 8, inner, 0)
        bias = bt[turn + 1]

        def conv(i, carry):
            x0 = i * 4
            left = jnp.concatenate(
                [
                    pad[pl.ds(x0 + dx, 4), dy : dy + 8].reshape(512, 384)
                    for dx in range(3)
                    for dy in range(3)
                ],
                axis=1,
            )
            out = jnp.dot(left, bw[turn + 1].reshape(3456, 256), preferred_element_type=F32)
            facc[pl.ds(i * 2, 2)] = (out + bias).reshape(2, 2, 4, 2, 16, 256)
            return carry

        lax.fori_loop(0, 2, conv, 0)

    def fine_fix(turn, moves):
        def one(pair):
            for f in pair:
                came(moves[f][0], moves[f][2])
            adds = []
            for f in pair:
                tap = 2 * (f % 2)
                cells_of = [blank]
                for k in range(8):
                    v = load_cell(fr, turn, f, k)
                    v = jnp.where(in_cross[f], take(v, index[f]), 0.0)
                    cells_of.append(pack6(v, zero8, zero8, low))
                cells_of.append(blank)
                lhs = jnp.concatenate(
                    [jnp.concatenate(cells_of[d : d + 8], axis=0) for d in range(3)], axis=1
                )
                taps = [3 * tap + d if f < 2 else 3 * d + tap for d in range(3)]
                rhs = jnp.concatenate([bw[turn + 1, k] for k in taps], axis=0)
                adds.append(
                    jnp.dot(lhs, rhs, preferred_element_type=F32).reshape(8, 16, 256)
                )
            for f, add in zip(pair, adds):
                k, h = 3 * (f % 2), f % 2
                if f < 2:
                    facc[k, h] = facc[k, h] + add.reshape(4, 2, 16, 256)
                else:
                    facc[:, :, k, h] = facc[:, :, k, h] + add.reshape(4, 2, 16, 256)

        by_parity(one)

    def add_to(x, y):
        return facc[x // 2, x % 2, y // 2, y % 2]

    def keep(x, y):
        s2[x, y] = jnp.maximum(add_to(x, y), 0.0).astype(BF)

    def final(x, y):
        v = jnp.maximum(add_to(x, y), 0.0)
        fout[:, (x * 8 + y) * 512 : (x * 8 + y + 1) * 512] = jnp.concatenate(
            [v[0:8], v[8:16]], axis=1
        ).astype(BF)

    for x in inside:
        for y in inside:
            begin(x, y)
    fine_main(s1, 0)
    parent_weights(vw.at[1], cu)
    fine_fix(0, moves)
    gives.wait_recv()
    parents = jnp.dot(sel2, precv[...].reshape(nc * 32, 256), preferred_element_type=F32)
    grown = [parents[q * 8 : (q + 1) * 8] for q in range(16)]
    for q in range(16):
        u = grown[q]
        ub[q // 4, q % 4] = jnp.concatenate([u[:, 0:128], u[:, 128:256]], axis=0).astype(BF)
    umoves = [face(ub, 3, fu, hsend, urecv, f) for f in range(4)]

    for q in range(16):
        u = grown[q]
        zm = jnp.where(local[4], take(u[:, 128:256], index[4]), 0.0)
        zp = jnp.where(local[5], take(u[:, 0:128], index[5]), 0.0)
        pu[q // 4 + 1, q % 4 + 1] = pack4(u, zm, zp, low)
    ublank = jnp.zeros((16, 256), BF)
    for i in (0, 5):
        for j in (0, 5):
            pu[i, j] = ublank
    for k in range(4):
        for f in range(4):
            at = 3 * (1 - f % 2)
            u = grown[at * 4 + k] if f < 2 else grown[k * 4 + at]
            half = in_local[f][:, 0:256]
            v = pack4(jnp.where(half, take(u, index[f]), 0.0), zero8, zero8, low)
            if f < 2:
                pu[5 * f, k + 1] = v
            else:
                pu[k + 1, 5 * (f - 2)] = v
    for px in range(2):
        for py in range(2):
            lhs = jnp.concatenate(
                [
                    pu[px + tx : px + tx + 4, py + ty : py + ty + 4].reshape(256, 256)
                    for tx in range(2)
                    for ty in range(2)
                ],
                axis=1,
            )
            out = jnp.dot(lhs, cu[px, py].reshape(1024, 256), preferred_element_type=F32)
            facc[:, px, :, py] = facc[:, px, :, py] + out.reshape(4, 4, 16, 256)
    build_weights(vw.at[2], bw.at[2])
    def up_fix(pair):
        for f in pair:
            came(umoves[f][0], umoves[f][2])
        adds = []
        for f in pair:
            tap = f % 2
            strip = [ublank]
            for k in range(4):
                v = fu[f, k].astype(F32)
                u = jnp.concatenate([v[0:8], v[8:16]], axis=1)
                u = jnp.where(in_cross[f][:, 0:256], take(u, index[f]), 0.0)
                strip.append(pack4(u, zero8, zero8, low))
            strip.append(ublank)
            for p in range(2):
                lhs = jnp.concatenate(
                    [jnp.concatenate(strip[p + t : p + t + 4], axis=0) for t in range(2)],
                    axis=1,
                )
                if f < 2:
                    rhs = cu[tap, p, tap].reshape(512, 256)
                else:
                    rhs = jnp.concatenate([cu[p, tap, t, tap] for t in range(2)], axis=0)
                add = jnp.dot(lhs, rhs, preferred_element_type=F32).reshape(4, 16, 256)
                adds.append((f, p, add))
        for f, p, add in adds:
            e, tap = 3 * (f % 2), f % 2
            if f < 2:
                facc[e, tap, :, p] = facc[e, tap, :, p] + add
            else:
                facc[:, p, e, tap] = facc[:, p, e, tap] + add

    by_parity(up_fix)
    for x in range(8):
        keep(x, 0)
        keep(x, 7)
    for y in inside:
        keep(0, y)
        keep(7, y)
    for copy, there, _ in moves:
        sent(copy, there)
    moves = [face(s2, 7, fr.at[1], fsend, frecv.at[1], f) for f in (2, 3, 0, 1)]
    moves = moves[2:] + moves[:2]
    for x in inside:
        for y in inside:
            keep(x, y)
    fine_main(s2, 1)
    for x in inside:
        for y in inside:
            final(x, y)
    fine_fix(1, moves)
    for x in range(8):
        final(x, 0)
        final(x, 7)
    for y in inside:
        final(0, y)
        final(7, y)
    for copy, there, _ in moves + umoves:
        sent(copy, there)
    asks.wait_send()
    gives.wait_send()


def put_out(coarse, fine, coarse_hbm, fine_hbm, sem):
    copies = []
    for k in range(PARTS):
        n = X // PARTS
        x = slice(k * n, (k + 1) * n)
        copies.append(pltpu.make_async_copy(coarse.at[x], coarse_hbm.at[x], sem.at[2 * k]))
        n = 32768 // PARTS
        x = slice(k * n, (k + 1) * n)
        copies.append(
            pltpu.make_async_copy(fine.at[:, x], fine_hbm.at[:, x], sem.at[2 * k + 1])
        )
    for copy in copies:
        copy.start()
    for copy in copies:
        copy.wait()


def shards(
    coarse_in,
    coarse_weight,
    coarse_bias,
    fine_in,
    weight_first,
    bias_first,
    weight_second,
    bias_second,
    parent_tile,
    parent_cell,
    neighbours,
):
    nr = lax.axis_size("row")
    nc = lax.axis_size("col")
    anywhere = pl.BlockSpec(memory_space=pl.ANY)
    vector = pl.BlockSpec(memory_space=pltpu.VMEM)
    dma = pltpu.SemaphoreType.DMA
    coarse, fine = pl.pallas_call(
        functools.partial(body, nr, nc),
        out_shape=(pltpu.VMEM(coarse_in.shape, BF), pltpu.VMEM(fine_in.shape, BF)),
        in_specs=[anywhere] * 11,
        out_specs=(vector, vector),
        scratch_shapes=[
            pltpu.SMEM((NB,), jnp.int32),
            pltpu.SMEM((NB,), jnp.int32),
            pltpu.SMEM((NB, 6), jnp.int32),
            pltpu.VMEM((3, 1, CH), F32),
            pltpu.VMEM((X, Y, 512), BF),
            pltpu.VMEM((NB, 32768), BF),
            pltpu.VMEM((3, 27, CH, CH), BF),
            pltpu.VMEM((3, 9, 384, 256), BF),
            pltpu.VMEM((3, 1, 256), F32),
            pltpu.VMEM((64, 512), BF),
            pltpu.VMEM((4, 1, 512), F32),
            pltpu.VMEM((2, 16, 512), BF),
            pltpu.VMEM((2, 32, 512), BF),
            pltpu.VMEM((4, 1, 512), F32),
            pltpu.VMEM((2, 2, 32, 256), F32),
            pltpu.VMEM((34, 2, 16, 1152), BF),
            pltpu.VMEM((X, 2, 16, 256), F32),
            pltpu.VMEM((X, 2, 16, 256), BF),
            pltpu.VMEM((nc, 1, 128), jnp.int32),
            pltpu.VMEM((nc, 1, 128), jnp.int32),
            pltpu.VMEM((nc, 32, 1024), BF),
            pltpu.VMEM((nc, 32, 256), BF),
            pltpu.VMEM((nc, 32, 256), BF),
            pltpu.VMEM((8, 8, 16, 256), BF),
            pltpu.VMEM((8, 8, 16, 256), BF),
            pltpu.VMEM((2, 4, 8, 16, 256), BF),
            pltpu.VMEM((10, 10, 16, 384), BF),
            pltpu.VMEM((4, 2, 4, 2, 16, 256), F32),
            pltpu.VMEM((2, 2, 2, 2, 256, 256), BF),
            pltpu.VMEM((4, 4, 16, 128), BF),
            pltpu.VMEM((4, 4, 16, 128), BF),
            pltpu.VMEM((6, 6, 16, 256), BF),
            dma((11,)),
            dma((8,)),
            dma((8,)),
            dma((2,)),
            dma((2,)),
            dma((4,)),
            dma((2, 4)),
            dma((4,)),
        ],
        compiler_params=pltpu.CompilerParams(collective_id=0, has_side_effects=True),
    )(
        coarse_in,
        coarse_weight,
        coarse_bias.reshape(1, CH),
        fine_in,
        weight_first,
        bias_first.reshape(1, CH),
        weight_second,
        bias_second.reshape(1, CH),
        parent_tile.reshape(NB),
        parent_cell,
        neighbours,
    )
    return pl.pallas_call(
        put_out,
        out_shape=(
            jax.ShapeDtypeStruct(coarse_in.shape, BF),
            jax.ShapeDtypeStruct(fine_in.shape, BF),
        ),
        in_specs=[anywhere, anywhere],
        out_specs=(anywhere, anywhere),
        scratch_shapes=[dma((2 * PARTS,))],
        compiler_params=pltpu.CompilerParams(vmem_limit_bytes=1 << 20),
    )(coarse, fine)


def solution(mesh):
    placed = (
        P("row", "col", None),
        P(),
        P(),
        P(("row", "col"), None),
        P(),
        P(),
        P(),
        P(),
        P(("row", "col"), None),
        P(("row", "col")),
        P(("row", "col"), None),
    )
    return jax.shard_map(
        shards,
        mesh=mesh,
        in_specs=placed,
        out_specs=(P("row", "col", None), P(("row", "col"), None)),
        check_vma=False,
    )
```

```python
import functools
import jax
import jax.numpy as jnp
from jax import lax
from jax.experimental import pallas as pl
from jax.experimental.pallas import tpu as pltpu
from jax.sharding import PartitionSpec as P

CH = 64
X = 32
Y = 16
NB = 8
CHUNKS = (2, 6, 8)
PARTS = 2
F32 = jnp.float32
BF = jnp.bfloat16
MESH = pl.DeviceIdType.MESH


def lanes(shape):
    return lax.broadcasted_iota(jnp.int32, shape, len(shape) - 1)


def sublanes(shape):
    return lax.broadcasted_iota(jnp.int32, shape, len(shape) - 2)


def build_weights(w, bw):
    zero = jnp.zeros((64, 64), BF)

    def one(k, carry):
        wm, w0, wp = w[3 * k], w[3 * k + 1], w[3 * k + 2]
        a = jnp.concatenate([w0, wm], axis=1)
        b = jnp.concatenate([wp, w0], axis=1)
        c = jnp.concatenate([zero, wp], axis=1)
        d = jnp.concatenate([wm, zero], axis=1)
        for r, v in enumerate((a, b, c)):
            bw[k, r * 64 : (r + 1) * 64, 0:128] = v
            bw[k, (r + 2) * 64 : (r + 3) * 64, 128:256] = v
        bw[k, 320:384, 0:128] = d
        bw[k, 64:128, 128:256] = d
        return carry

    lax.fori_loop(0, 9, one, 0, unroll=9)


def blank_weights(bw):
    wide = jnp.zeros((64, 128), BF)

    def one(k, carry):
        for i in range(3):
            for r, at in ((0, 128), (3, 0), (4, 0), (5, 128)):
                bw[i, k, r * 64 : (r + 1) * 64, at : at + 128] = wide
        return carry

    lax.fori_loop(0, 9, one, 0)


def parent_weights(w, cu):
    zero = jnp.zeros((64, 64), BF)
    wide = jnp.zeros((64, 128), BF)
    taps = {(0, 0): (0,), (0, 1): (1, 2), (1, 0): (0, 1), (1, 1): (2,)}
    xs = {}
    for key in taps:
        for k in range(9):
            xs[key, k] = sum(w[9 * d + k].astype(F32) for d in taps[key])
    for px, tx in taps:
        for py, ty in taps:
            t = [
                sum(xs[(px, tx), 3 * d + z] for d in taps[py, ty]) for z in range(3)
            ]
            a, b, d, e = [v.astype(BF) for v in (t[0], t[0] + t[1], t[1] + t[2], t[2])]
            one = jnp.concatenate([d, b], axis=1)
            two = jnp.concatenate([zero, e], axis=1)
            three = jnp.concatenate([a, zero], axis=1)
            for r, (left, right) in enumerate(
                ((one, three), (two, one), (wide, two), (three, wide))
            ):
                cu[px, py, tx, ty, r * 64 : (r + 1) * 64, 0:128] = left
                cu[px, py, tx, ty, r * 64 : (r + 1) * 64, 128:256] = right


def tile_bias(b, bt):
    for i in range(4):
        bt[:, i * 64 : (i + 1) * 64] = b[...]


def take(v, idx):
    return jnp.concatenate(
        [
            jnp.take_along_axis(v[:, k : k + 128], idx, axis=0, mode="promise_in_bounds")
            for k in range(0, v.shape[1], 128)
        ],
        axis=1,
    )


def pack6(v, zm, zp, low):
    first = jnp.concatenate([v[:, 0:256], jnp.where(low, v[:, 256:384], zm)], axis=1)
    second = jnp.concatenate([v[:, 256:512], jnp.where(low, zp, v[:, 128:256])], axis=1)
    return jnp.concatenate([first, second], axis=0).astype(BF)


def pack4(u, zm, zp, low):
    first = jnp.concatenate([u[:, 0:128], jnp.where(low, u[:, 128:256], zm)], axis=1)
    second = jnp.concatenate([u[:, 128:256], jnp.where(low, zp, u[:, 0:128])], axis=1)
    return jnp.concatenate([first, second], axis=0).astype(BF)


def load_cell(s, *at):
    v = s[at].astype(F32)
    return jnp.concatenate([v[0:8], v[8:16]], axis=1)


def order(nc):
    side = {16: 4, 4: 2}[nc]
    dist = lambda v: min(v, side - v)
    pairs = [(a, b) for a in range(side) for b in range(side)]
    return side, sorted(pairs, key=lambda p: -dist(p[0]) - dist(p[1]))


def body(
    nr,
    nc,
    cin,
    cw,
    cb,
    fin,
    w1,
    b1,
    w2,
    b2,
    ptile_in,
    pcell_in,
    nb_in,
    cout,
    fout,
    ptile,
    pcell,
    nb,
    braw,
    vin,
    vf,
    vw,
    bw,
    bt,
    edge,
    crn,
    hx,
    hy,
    hc,
    yl,
    cp,
    cacc,
    cs,
    req,
    reqr,
    sel,
    psend,
    precv,
    s1,
    s2,
    fr,
    pad,
    facc,
    cu,
    ub,
    fu,
    pu,
    lsem,
    hsend,
    hrecv,
    asem,
    gsem,
    fsend,
    frecv,
    urecv,
):
    r = lax.axis_index("row")
    c = lax.axis_index("col")
    me = r * nc + c
    side, offsets = order(nc)
    cy, cz = lax.div(c, side), lax.rem(c, side)
    peers = [lax.rem(cy + a, side) * side + lax.rem(cz + b, side) for a, b in offsets]
    up, down, right, left = r < nr - 1, r > 0, c < nc - 1, c > 0
    barrier = pltpu.get_barrier_semaphore()
    near = [
        ((r, c + 1), right),
        ((r, c - 1), left),
        ((r + 1, c), up),
        ((r - 1, c), down),
        ((r + 1, c + 1), up & right),
        ((r + 1, c - 1), up & left),
        ((r - 1, c + 1), down & right),
        ((r - 1, c - 1), down & left),
    ]
    heard = jnp.int32(nc - 1)
    for d in peers[:-1]:
        pl.semaphore_signal(barrier, inc=1, device_id=(r, d), device_id_type=MESH)
    for peer, there in near[2:]:
        heard = heard + jnp.where(there, 1, 0)

        @pl.when(there)
        def _(peer=peer):
            pl.semaphore_signal(barrier, inc=1, device_id=peer, device_id_type=MESH)

    loads = [
        pltpu.make_async_copy(cin, vin, lsem.at[0]),
        pltpu.make_async_copy(ptile_in, ptile, lsem.at[5]),
        pltpu.make_async_copy(pcell_in, pcell, lsem.at[6]),
        pltpu.make_async_copy(cw, vw.at[0], lsem.at[1]),
        pltpu.make_async_copy(nb_in, nb, lsem.at[7]),
        pltpu.make_async_copy(cb, braw.at[0], lsem.at[8]),
        pltpu.make_async_copy(b1, braw.at[1], lsem.at[9]),
        pltpu.make_async_copy(b2, braw.at[2], lsem.at[10]),
        pltpu.make_async_copy(fin, vf, lsem.at[2]),
        pltpu.make_async_copy(w1, vw.at[1], lsem.at[3]),
        pltpu.make_async_copy(w2, vw.at[2], lsem.at[4]),
    ]
    lin, ltile, lcell, lcw, lnb, lb0, lb1, lb2, lfin, lw1, lw2 = loads
    for copy in loads:
        copy.start()

    def remote(src, dst, ssem, rsem, peer):
        return pltpu.make_async_remote_copy(
            src_ref=src,
            dst_ref=dst,
            send_sem=ssem,
            recv_sem=rsem,
            device_id=peer,
            device_id_type=MESH,
        )

    def start(copy, there):
        @pl.when(there)
        def _():
            copy.start()

    def sent(copy, there):
        @pl.when(there)
        def _():
            copy.wait_send()

    def came(copy, there):
        @pl.when(there)
        def _():
            copy.wait_recv()
    ei = sublanes((64, 512))
    ej = lanes((64, 512))
    pick = jnp.where(ej == jnp.where(ei < 32, ei * 16 + 15, (ei - 32) * 16), 1.0, 0.0).astype(BF)
    blank_weights(bw)
    ltile.wait()
    lcell.wait()
    tiles = [ptile[b] for b in range(NB)]
    cells = [pcell[b] for b in range(NB)]
    slots = []
    for b in range(NB):
        n = jnp.int32(0)
        for e in range(b):
            n = n + jnp.where(tiles[e] == tiles[b], 1, 0)
        slots.append(n)
    row_id = sublanes((nc, 128))
    wanted = jnp.zeros((nc, 128), jnp.int32)
    for b in range(NB):
        ask = (cells[b] + 1) * jnp.where(slots[b] == 0, 1, 128)
        wanted = wanted + jnp.where(row_id == tiles[b], ask, 0)
    for t in range(nc):
        req[t] = wanted[t : t + 1]

    lin.wait()
    found = jnp.dot(pick, vin[...].reshape(512, 512), preferred_element_type=F32)
    edge[...] = found.astype(BF)
    for i, row in enumerate((31, 63, 0, 32)):
        crn[i] = found[row : row + 1]
    lcw.wait()
    build_weights(vw.at[0], bw.at[0])
    lb0.wait()
    lb1.wait()
    lb2.wait()
    for i in range(3):
        tile_bias(braw.at[i], bt.at[i])
    pl.semaphore_wait(barrier, heard)
    for d in peers[:-1]:
        remote(req.at[d], reqr.at[c], asem.at[0], asem.at[1], (r, d)).start()
    asks = remote(
        req.at[pl.ds(0, nc - 1)],
        reqr.at[pl.ds(0, nc - 1)],
        asem.at[0],
        asem.at[1],
        (r, peers[0]),
    )
    halos = []
    for i, (src, dst, to, frm) in enumerate(
        (
            (crn.at[0], hc.at[0], 4, 7),
            (crn.at[1], hc.at[1], 5, 6),
            (crn.at[2], hc.at[2], 6, 5),
            (crn.at[3], hc.at[3], 7, 4),
            (edge.at[0:32], hy.at[0], 0, 1),
            (edge.at[32:64], hy.at[1], 1, 0),
            (vin.at[31], hx.at[0], 2, 3),
            (vin.at[0], hx.at[1], 3, 2),
        )
    ):
        copy = remote(src, dst, hsend.at[i], hrecv.at[i], near[to][0])
        start(copy, near[to][1])
        halos.append((copy, near[to][1], near[frm][1]))
    reqr[c] = req[c]

    def face(s, last, dst, ssem, rsem, f):
        src = s.at[last if f == 0 else 0] if f < 2 else s.at[:, last if f == 2 else 0]
        to, frm = ((2, 3), (3, 2), (0, 1), (1, 0))[f]
        copy = remote(src, dst.at[f], ssem.at[f], rsem.at[f], near[to][0])
        start(copy, near[to][1])
        return copy, near[to][1], near[frm][1]

    def begin(x, y):
        o = (x * 8 + y) * 512
        v = vf[:, o : o + 512].astype(F32)
        s1[x, y] = jnp.concatenate([v[:, 0:256], v[:, 256:512]], axis=0).astype(BF)

    inside = range(1, 7)
    lfin.wait()
    for x in range(8):
        begin(x, 0)
        begin(x, 7)
    for y in inside:
        begin(0, y)
        begin(7, y)
    moves = [face(s1, 7, fr.at[0], fsend, frecv.at[0], f) for f in range(4)]

    low16 = lanes((16, 128)) < 64
    zero16 = jnp.zeros((16, 128), F32)
    y16 = sublanes((16, 512))

    def place(at, a, left, right):
        for dy, v in enumerate(
            (
                jnp.where(y16 == 0, left, pltpu.roll(a, 1, 0)),
                a,
                jnp.where(y16 == 15, right, pltpu.roll(a, 15, 0)),
            )
        ):
            o = dy * 384
            cp[at, 0, :, o : o + 256] = v[:, 0:256].astype(BF)
            cp[at, 0, :, o + 256 : o + 384] = jnp.where(low16, v[:, 256:384], zero16).astype(BF)
            cp[at, 1, :, o : o + 256] = v[:, 256:512].astype(BF)
            cp[at, 1, :, o + 256 : o + 384] = jnp.where(low16, zero16, v[:, 128:256]).astype(BF)

    def coarse_one(x, carry):
        place(x + 1, vin[x].astype(F32), 0.0, 0.0)
        return carry

    lax.fori_loop(0, X, coarse_one, 0)
    blank = jnp.zeros((2, 16, 1152), BF)
    cp[0] = blank
    cp[33] = blank
    cbias = bt[0]

    def coarse_conv(i, carry):
        x0 = i * 16
        left = jnp.concatenate(
            [cp[pl.ds(x0 + dx, 16)].reshape(512, 1152) for dx in range(3)], axis=1
        )
        out = jnp.dot(left, bw[0].reshape(3456, 256), preferred_element_type=F32)
        cacc[pl.ds(x0, 16)] = (out + cbias).reshape(16, 2, 16, 256)
        return carry

    lax.fori_loop(0, 2, coarse_conv, 0)
    for copy, _, there in halos:
        came(copy, there)

    for at, ok, i, j in ((0, down, 0, 0), (33, up, 1, 2)):
        place(
            at,
            jnp.where(ok, hx[i].astype(F32), 0.0),
            jnp.where(ok & left, hc[j], 0.0),
            jnp.where(ok & right, hc[j + 1], 0.0),
        )
    low32 = lanes((32, 128)) < 64
    x32 = sublanes((32, 256))
    for i, ok in enumerate((left, right)):
        v = jnp.where(ok, hy[i].astype(F32), 0.0)
        lhs = jnp.concatenate(
            [
                jnp.concatenate([v[:, 0:256], jnp.where(low32, v[:, 256:384], 0.0)], axis=1),
                jnp.concatenate([v[:, 256:512], jnp.where(low32, 0.0, v[:, 128:256])], axis=1),
            ],
            axis=0,
        ).astype(BF)
        part = [
            jnp.dot(lhs, bw[0, 3 * dx + 2 * i], preferred_element_type=F32) for dx in range(3)
        ]
        for g in range(2):
            before, here, after = [p[g * 32 : (g + 1) * 32] for p in part]
            yl[i, g] = (
                here
                + jnp.where(x32 == 0, 0.0, pltpu.roll(before, 1, 0))
                + jnp.where(x32 == 31, 0.0, pltpu.roll(after, 31, 0))
            )
    for at, x, k in ((0, 0, 0), (33, 31, 6)):
        cacc[x] = cacc[x] + jnp.dot(
            cp[at].reshape(32, 1152),
            bw[0, k : k + 3].reshape(1152, 256),
            preferred_element_type=F32,
        ).reshape(2, 16, 256)
    y256 = sublanes((16, 256))

    def coarse_out(x, carry):
        for g in range(2):
            v = cacc[x, g]
            v = v + jnp.where(y256 == 0, yl[0, g, pl.ds(x, 1), :], 0.0)
            v = v + jnp.where(y256 == 15, yl[1, g, pl.ds(x, 1), :], 0.0)
            v = jnp.maximum(v, 0.0).astype(BF)
            cs[x, g] = v
            cout[x, :, g * 256 : (g + 1) * 256] = v
        return carry

    lax.fori_loop(0, X, coarse_out, 0, unroll=2)

    asks.wait_recv()
    i16 = sublanes((16, 128))
    l16 = lanes((16, 128))
    def choose(k, d):
        both = jnp.broadcast_to(reqr[d], (16, 128))
        for s in range(2):
            cell = ((both >> (7 * s)) & 127) - 1
            px = (cell >> 3) * 4 + (i16 >> 2)
            py = ((cell >> 1) & 3) * 4 + (i16 & 3)
            target = jnp.where(cell >= 0, (px * 2 + (cell & 1)) * 16 + py, -1)
            for j in range(8):
                sel[k, s * 16 : (s + 1) * 16, j * 128 : (j + 1) * 128] = jnp.where(
                    target == l16 + j * 128, 1.0, 0.0
                ).astype(BF)
    m = 0
    for n in CHUNKS if nc == 16 else (nc,):
        for k in range(m, m + n):
            choose(k, peers[k])
        psend[m : m + n] = (
            jnp.dot(
                sel[m : m + n].reshape(n * 32, 1024),
                cs[...].reshape(1024, 256),
                preferred_element_type=F32,
            )
            .astype(BF)
            .reshape(n, 32, 256)
        )
        for k in range(m, m + n):
            if k < nc - 1:
                remote(
                    psend.at[k], precv.at[c], gsem.at[0], gsem.at[1], (r, peers[k])
                ).start()
        m += n
    gives = remote(
        psend.at[pl.ds(0, nc - 1)],
        precv.at[pl.ds(0, nc - 1)],
        gsem.at[0],
        gsem.at[1],
        (r, peers[0]),
    )
    precv[c] = psend[nc - 1]
    lw1.wait()
    build_weights(vw.at[1], bw.at[1])
    lw2.wait()
    lnb.wait()
    b8 = sublanes((8, 128))
    low = lanes((8, 128)) < 64
    index, local, cross = [], [], []
    for f in range(6):
        linked = jnp.full((8, 128), -1, jnp.int32)
        for b in range(NB):
            linked = jnp.where(b8 == b, nb[b, f], linked)
        owner = linked >> 3
        index.append(linked & 7)
        local.append(owner == me)
        other = me + (-nc, nc, -1, 1, -1, 1)[f]
        cross.append((linked >= 0) & (owner == other))

    base = jnp.zeros((8, 128), jnp.int32)
    for b in range(NB):
        base = jnp.where(b8 == b, tiles[b] * 32 + slots[b] * 16, base)
    l8 = lanes((8, 128))
    rows = []
    for q in range(16):
        rows.append(
            jnp.concatenate(
                [
                    jnp.where(base + q == l8 + k * 128, 1.0, 0.0)
                    for k in range(nc * 32 // 128)
                ],
                axis=1,
            )
        )
    sel2 = jnp.concatenate(rows, axis=0).astype(BF)

    zero8 = jnp.zeros((8, 128), F32)
    blank = jnp.zeros((16, 384), BF)
    for i in (0, 9):
        for j in (0, 9):
            pad[i, j] = blank
    in_local = [jnp.concatenate([m] * 4, axis=1) for m in local[:4]]
    in_cross = [jnp.concatenate([m] * 4, axis=1) for m in cross[:4]]
    for copy, there, _ in halos:
        sent(copy, there)

    def by_parity(one):
        @pl.when(lax.rem(r, 2) == 0)
        def _():
            one((0, 1))

        one((2, 3))

        @pl.when(lax.rem(r, 2) == 1)
        def _():
            one((0, 1))

    def fine_main(s, turn):
        def inner(x, carry):
            for y in range(8):
                v = load_cell(s, x, y)
                zm = jnp.where(local[4], take(v[:, 384:512], index[4]), 0.0)
                zp = jnp.where(local[5], take(v[:, 0:128], index[5]), 0.0)
                pad[x + 1, y + 1] = pack6(v, zm, zp, low)
            for f in range(4):
                k = 7 if f % 2 == 0 else 0
                v = load_cell(s, k, x) if f < 2 else load_cell(s, x, k)
                v = pack6(jnp.where(in_local[f], take(v, index[f]), 0.0), zero8, zero8, low)
                if f < 2:
                    pad[9 * f, x + 1] = v
                else:
                    pad[x + 1, 9 * (f - 2)] = v
            return carry

        lax.fori_loop(0, 8, inner, 0)
        bias = bt[turn + 1]

        def conv(i, carry):
            x0 = i * 4
            left = jnp.concatenate(
                [
                    pad[pl.ds(x0 + dx, 4), dy : dy + 8].reshape(512, 384)
                    for dx in range(3)
                    for dy in range(3)
                ],
                axis=1,
            )
            out = jnp.dot(left, bw[turn + 1].reshape(3456, 256), preferred_element_type=F32)
            facc[pl.ds(i * 2, 2)] = (out + bias).reshape(2, 2, 4, 2, 16, 256)
            return carry

        lax.fori_loop(0, 2, conv, 0)

    def fine_fix(turn, moves):
        def one(pair):
            for f in pair:
                came(moves[f][0], moves[f][2])
            adds = []
            for f in pair:
                tap = 2 * (f % 2)
                cells_of = [blank]
                for k in range(8):
                    v = load_cell(fr, turn, f, k)
                    v = jnp.where(in_cross[f], take(v, index[f]), 0.0)
                    cells_of.append(pack6(v, zero8, zero8, low))
                cells_of.append(blank)
                lhs = jnp.concatenate(
                    [jnp.concatenate(cells_of[d : d + 8], axis=0) for d in range(3)], axis=1
                )
                taps = [3 * tap + d if f < 2 else 3 * d + tap for d in range(3)]
                rhs = jnp.concatenate([bw[turn + 1, k] for k in taps], axis=0)
                adds.append(
                    jnp.dot(lhs, rhs, preferred_element_type=F32).reshape(8, 16, 256)
                )
            for f, add in zip(pair, adds):
                k, h = 3 * (f % 2), f % 2
                if f < 2:
                    facc[k, h] = facc[k, h] + add.reshape(4, 2, 16, 256)
                else:
                    facc[:, :, k, h] = facc[:, :, k, h] + add.reshape(4, 2, 16, 256)

        by_parity(one)

    def add_to(x, y):
        return facc[x // 2, x % 2, y // 2, y % 2]

    def keep(x, y):
        s2[x, y] = jnp.maximum(add_to(x, y), 0.0).astype(BF)

    def final(x, y):
        v = jnp.maximum(add_to(x, y), 0.0)
        fout[:, (x * 8 + y) * 512 : (x * 8 + y + 1) * 512] = jnp.concatenate(
            [v[0:8], v[8:16]], axis=1
        ).astype(BF)

    for x in inside:
        for y in inside:
            begin(x, y)
    fine_main(s1, 0)
    parent_weights(vw.at[1], cu)
    fine_fix(0, moves)

    build_weights(vw.at[2], bw.at[2])
    gives.wait_recv()
    parents = jnp.dot(sel2, precv[...].reshape(nc * 32, 256), preferred_element_type=F32)
    grown = [parents[q * 8 : (q + 1) * 8] for q in range(16)]
    for q in range(16):
        u = grown[q]
        ub[q // 4, q % 4] = jnp.concatenate([u[:, 0:128], u[:, 128:256]], axis=0).astype(BF)
    umoves = [face(ub, 3, fu, hsend, urecv, f) for f in range(4)]

    for q in range(16):
        u = grown[q]
        zm = jnp.where(local[4], take(u[:, 128:256], index[4]), 0.0)
        zp = jnp.where(local[5], take(u[:, 0:128], index[5]), 0.0)
        pu[q // 4 + 1, q % 4 + 1] = pack4(u, zm, zp, low)
    ublank = jnp.zeros((16, 256), BF)
    for i in (0, 5):
        for j in (0, 5):
            pu[i, j] = ublank
    for k in range(4):
        for f in range(4):
            at = 3 * (1 - f % 2)
            u = grown[at * 4 + k] if f < 2 else grown[k * 4 + at]
            half = in_local[f][:, 0:256]
            v = pack4(jnp.where(half, take(u, index[f]), 0.0), zero8, zero8, low)
            if f < 2:
                pu[5 * f, k + 1] = v
            else:
                pu[k + 1, 5 * (f - 2)] = v
    for px in range(2):
        for py in range(2):
            lhs = jnp.concatenate(
                [
                    pu[px + tx : px + tx + 4, py + ty : py + ty + 4].reshape(256, 256)
                    for tx in range(2)
                    for ty in range(2)
                ],
                axis=1,
            )
            out = jnp.dot(lhs, cu[px, py].reshape(1024, 256), preferred_element_type=F32)
            facc[:, px, :, py] = facc[:, px, :, py] + out.reshape(4, 4, 16, 256)

    def up_fix(pair):
        for f in pair:
            came(umoves[f][0], umoves[f][2])
        adds = []
        for f in pair:
            tap = f % 2
            strip = [ublank]
            for k in range(4):
                v = fu[f, k].astype(F32)
                u = jnp.concatenate([v[0:8], v[8:16]], axis=1)
                u = jnp.where(in_cross[f][:, 0:256], take(u, index[f]), 0.0)
                strip.append(pack4(u, zero8, zero8, low))
            strip.append(ublank)
            for p in range(2):
                lhs = jnp.concatenate(
                    [jnp.concatenate(strip[p + t : p + t + 4], axis=0) for t in range(2)],
                    axis=1,
                )
                if f < 2:
                    rhs = cu[tap, p, tap].reshape(512, 256)
                else:
                    rhs = jnp.concatenate([cu[p, tap, t, tap] for t in range(2)], axis=0)
                add = jnp.dot(lhs, rhs, preferred_element_type=F32).reshape(4, 16, 256)
                adds.append((f, p, add))
        for f, p, add in adds:
            e, tap = 3 * (f % 2), f % 2
            if f < 2:
                facc[e, tap, :, p] = facc[e, tap, :, p] + add
            else:
                facc[:, p, e, tap] = facc[:, p, e, tap] + add

    by_parity(up_fix)
    for x in range(8):
        keep(x, 0)
        keep(x, 7)
    for y in inside:
        keep(0, y)
        keep(7, y)
    for copy, there, _ in moves:
        sent(copy, there)
    moves = [face(s2, 7, fr.at[1], fsend, frecv.at[1], f) for f in (2, 3, 0, 1)]
    moves = moves[2:] + moves[:2]
    for x in inside:
        for y in inside:
            keep(x, y)
    fine_main(s2, 1)
    for x in inside:
        for y in inside:
            final(x, y)
    fine_fix(1, moves)
    for x in range(8):
        final(x, 0)
        final(x, 7)
    for y in inside:
        final(0, y)
        final(7, y)
    for copy, there, _ in moves + umoves:
        sent(copy, there)
    asks.wait_send()
    gives.wait_send()


def put_out(coarse, fine, coarse_hbm, fine_hbm, sem):
    copies = []
    for k in range(PARTS):
        n = X // PARTS
        x = slice(k * n, (k + 1) * n)
        copies.append(pltpu.make_async_copy(coarse.at[x], coarse_hbm.at[x], sem.at[2 * k]))
        n = 32768 // PARTS
        x = slice(k * n, (k + 1) * n)
        copies.append(
            pltpu.make_async_copy(fine.at[:, x], fine_hbm.at[:, x], sem.at[2 * k + 1])
        )
    for copy in copies:
        copy.start()
    for copy in copies:
        copy.wait()


def shards(
    coarse_in,
    coarse_weight,
    coarse_bias,
    fine_in,
    weight_first,
    bias_first,
    weight_second,
    bias_second,
    parent_tile,
    parent_cell,
    neighbours,
):
    nr = lax.axis_size("row")
    nc = lax.axis_size("col")
    anywhere = pl.BlockSpec(memory_space=pl.ANY)
    vector = pl.BlockSpec(memory_space=pltpu.VMEM)
    dma = pltpu.SemaphoreType.DMA
    coarse, fine = pl.pallas_call(
        functools.partial(body, nr, nc),
        out_shape=(pltpu.VMEM(coarse_in.shape, BF), pltpu.VMEM(fine_in.shape, BF)),
        in_specs=[anywhere] * 11,
        out_specs=(vector, vector),
        scratch_shapes=[
            pltpu.SMEM((NB,), jnp.int32),
            pltpu.SMEM((NB,), jnp.int32),
            pltpu.SMEM((NB, 6), jnp.int32),
            pltpu.VMEM((3, 1, CH), F32),
            pltpu.VMEM((X, Y, 512), BF),
            pltpu.VMEM((NB, 32768), BF),
            pltpu.VMEM((3, 27, CH, CH), BF),
            pltpu.VMEM((3, 9, 384, 256), BF),
            pltpu.VMEM((3, 1, 256), F32),
            pltpu.VMEM((64, 512), BF),
            pltpu.VMEM((4, 1, 512), F32),
            pltpu.VMEM((2, 16, 512), BF),
            pltpu.VMEM((2, 32, 512), BF),
            pltpu.VMEM((4, 1, 512), F32),
            pltpu.VMEM((2, 2, 32, 256), F32),
            pltpu.VMEM((34, 2, 16, 1152), BF),
            pltpu.VMEM((X, 2, 16, 256), F32),
            pltpu.VMEM((X, 2, 16, 256), BF),
            pltpu.VMEM((nc, 1, 128), jnp.int32),
            pltpu.VMEM((nc, 1, 128), jnp.int32),
            pltpu.VMEM((nc, 32, 1024), BF),
            pltpu.VMEM((nc, 32, 256), BF),
            pltpu.VMEM((nc, 32, 256), BF),
            pltpu.VMEM((8, 8, 16, 256), BF),
            pltpu.VMEM((8, 8, 16, 256), BF),
            pltpu.VMEM((2, 4, 8, 16, 256), BF),
            pltpu.VMEM((10, 10, 16, 384), BF),
            pltpu.VMEM((4, 2, 4, 2, 16, 256), F32),
            pltpu.VMEM((2, 2, 2, 2, 256, 256), BF),
            pltpu.VMEM((4, 4, 16, 128), BF),
            pltpu.VMEM((4, 4, 16, 128), BF),
            pltpu.VMEM((6, 6, 16, 256), BF),
            dma((11,)),
            dma((8,)),
            dma((8,)),
            dma((2,)),
            dma((2,)),
            dma((4,)),
            dma((2, 4)),
            dma((4,)),
        ],
        compiler_params=pltpu.CompilerParams(collective_id=0, has_side_effects=True),
    )(
        coarse_in,
        coarse_weight,
        coarse_bias.reshape(1, CH),
        fine_in,
        weight_first,
        bias_first.reshape(1, CH),
        weight_second,
        bias_second.reshape(1, CH),
        parent_tile.reshape(NB),
        parent_cell,
        neighbours,
    )
    return pl.pallas_call(
        put_out,
        out_shape=(
            jax.ShapeDtypeStruct(coarse_in.shape, BF),
            jax.ShapeDtypeStruct(fine_in.shape, BF),
        ),
        in_specs=[anywhere, anywhere],
        out_specs=(anywhere, anywhere),
        scratch_shapes=[dma((2 * PARTS,))],
        compiler_params=pltpu.CompilerParams(vmem_limit_bytes=1 << 20),
    )(coarse, fine)


def solution(mesh):
    placed = (
        P("row", "col", None),
        P(),
        P(),
        P(("row", "col"), None),
        P(),
        P(),
        P(),
        P(),
        P(("row", "col"), None),
        P(("row", "col")),
        P(("row", "col"), None),
    )
    return jax.shard_map(
        shards,
        mesh=mesh,
        in_specs=placed,
        out_specs=(P("row", "col", None), P(("row", "col"), None)),
        check_vma=False,
    )
```
